256 devices in a mesh: ctx: 32 (over z, y), tp: 4 (over x), fsdp: 2 (over core).
Axes of the slice: x: 4, y: 4, z: 8, core: 2. Of those that a mesh axis runs over, the one named last changes fastest.
Arguments:
- tokens: bfloat16 [2, 32768, 2048], P('fsdp', 'ctx'), may hold values from -6 to 6
- query_weight: bfloat16 [2048, 2048], P('fsdp', 'tp'), may hold values from -0.125 to 0.125
- key_weight: bfloat16 [2048, 2048], P('fsdp', 'tp'), may hold values from -0.125 to 0.125
- value_weight: bfloat16 [2048, 2048], P('fsdp', 'tp'), may hold values from -0.125 to 0.125
- gate_weight: bfloat16 [2048, 2048], P('fsdp', 'tp'), may hold values from -0.125 to 0.125
- out_weight: bfloat16 [2048, 2048], P('tp', 'fsdp'), may hold values from -0.125 to 0.125
- log_decay: float32 [2, 32768, 8], P('fsdp', 'ctx', 'tp'), may hold values from -1 to 0
Outputs:
- mixed: bfloat16 [2, 32768, 2048], P('fsdp', 'ctx', 'tp')
The draws below stay inside these ranges and needn't reach their ends.
All inputs are finite; a program needn't handle non-finite values.
Results may differ from the reference program's by a relative error of at most 0.013.
Values may be sent and summed in bfloat16 or wider, within the bound.
A program may use at most 128 MiB of HBM per device.

```python
import jax
import jax.numpy as jnp
from jax import lax

D = 2048
RETENTION_HEADS = 8
DH = 256
BLOCK = 512
TOK_DEV = 1024
SEQUENCE_COUNT = 2
SEQUENCE_LENGTH = 32768


def draw_log_decay(key, part):
    head_order = jax.random.permutation(jax.random.fold_in(key, 11), RETENTION_HEADS)
    fast_count = RETENTION_HEADS // 2
    fast_heads = head_order < fast_count
    fast_rate = jnp.exp(jax.random.uniform(jax.random.fold_in(key, 12), (RETENTION_HEADS,), jnp.float32, jnp.log(1.0 / 50.0), jnp.log(1.0 / 30.0)))
    slow_low = jnp.log(jnp.float32(0.05) / SEQUENCE_LENGTH)
    slow_high = jnp.log(jnp.float32(0.25) / SEQUENCE_LENGTH)
    slow_rate = jnp.exp(jax.random.uniform(jax.random.fold_in(key, 13), (RETENTION_HEADS,), jnp.float32, slow_low, slow_high))
    baseline_rate = jnp.where(fast_heads, fast_rate, slow_rate)
    device_multiplier = jnp.exp(jax.random.uniform(jax.random.fold_in(key, 14), (SEQUENCE_COUNT, SEQUENCE_LENGTH // TOK_DEV, 1, RETENTION_HEADS), jnp.float32, jnp.log(0.5), jnp.log(2.0)))
    device_multiplier = jnp.repeat(device_multiplier, TOK_DEV, axis=2).reshape(SEQUENCE_COUNT, SEQUENCE_LENGTH, RETENTION_HEADS)
    token_multiplier = jax.random.uniform(jax.random.fold_in(key, 15), (SEQUENCE_COUNT, SEQUENCE_LENGTH, RETENTION_HEADS), jnp.float32, 0.5, 1.5)
    spike_first_index = jax.random.randint(jax.random.fold_in(key, 16), (SEQUENCE_COUNT, 1), 0, SEQUENCE_LENGTH)
    spike_stride = jax.random.randint(jax.random.fold_in(key, 18), (SEQUENCE_COUNT, 1), 1, SEQUENCE_LENGTH)
    spike_positions = jnp.concatenate([spike_first_index, (spike_first_index + spike_stride) % SEQUENCE_LENGTH], axis=1)
    spike_penalty = jax.random.uniform(jax.random.fold_in(key, 17), (SEQUENCE_COUNT, 2, RETENTION_HEADS), jnp.float32, 0.2, 0.5)
    spike_hit_count = jnp.arange(SEQUENCE_LENGTH)[None, :, None] == spike_positions[:, None, :]
    spike_total_sum = jnp.sum(jnp.where(spike_hit_count[..., None], jnp.log(1.0 - spike_penalty)[:, None, :, :], 0.0), axis=2)
    return -baseline_rate[None, None, :] * device_multiplier * token_multiplier + spike_total_sum


def shard_levels(key, shape, pieces, low, largest):
    factor_of, own = 1.0, jax.random.fold_in(key, 6)
    for dim, shards_of in pieces:
        heights = jnp.exp(jax.random.uniform(jax.random.fold_in(own, dim), (shards_of,), jnp.float32, low / len(pieces), largest / len(pieces)))
        factor_of = factor_of * jnp.repeat(heights, shape[dim] // shards_of).reshape([-1 if axis == dim else 1 for axis in range(len(shape))])
    return factor_of


def scatter_about(rng, extent, deviation, limit, cuts=(), dtype=jnp.bfloat16):
    values = deviation * jax.random.normal(rng, extent, jnp.float32)
    if cuts:
        values = values * shard_levels(rng, extent, cuts, -0.22, 0.18)
    return jnp.clip(values, -limit, limit).astype(dtype)


def setup_inputs(seed: int = 0) -> dict:
    arg_keys = jax.random.split(jax.random.key(seed), 8)
    tokens = scatter_about(arg_keys[0], (SEQUENCE_COUNT, SEQUENCE_LENGTH, D), 1.0, 6.0, ((0, 2), (1, 32)))
    query_weight = scatter_about(arg_keys[1], (D, D), D ** -0.5, 0.125, ((0, 2), (1, 4)))
    key_weight = scatter_about(arg_keys[2], (D, D), D ** -0.5, 0.125, ((0, 2), (1, 4)))
    value_weight = scatter_about(arg_keys[3], (D, D), D ** -0.5, 0.125, ((0, 2), (1, 4)))
    gate_weight = scatter_about(arg_keys[4], (D, D), D ** -0.5, 0.125, ((0, 2), (1, 4)))
    out_weight = scatter_about(arg_keys[5], (D, D), D ** -0.5, 0.125, ((0, 4), (1, 2)))
    log_decay = draw_log_decay(jax.random.fold_in(arg_keys[7], 71), 0)
    return {"tokens": tokens, "query_weight": query_weight, "key_weight": key_weight, "value_weight": value_weight, "gate_weight": gate_weight, "out_weight": out_weight, "log_decay": log_decay}


def rotate(values, positions):
    half_dim = values.shape[-1] // 2
    index_row = jnp.arange(half_dim).astype(jnp.float32)
    frequency = jnp.power(jnp.float32(10000.0), -index_row / half_dim)
    angles = positions[:, None] * frequency[None, :]
    cosine = jnp.concatenate([jnp.cos(angles), jnp.cos(angles)], axis=-1)[:, None, :]
    sine_part = jnp.concatenate([jnp.sin(angles), jnp.sin(angles)], axis=-1)[:, None, :]
    turned = jnp.concatenate([-values[..., half_dim:], values[..., :half_dim]], axis=-1)
    return values * cosine + turned * sine_part

def group_norm(retained):
    center = retained - lax.optimization_barrier(jnp.mean(retained, axis=-1, keepdims=True))
    spread = lax.optimization_barrier(jnp.mean(center * center, axis=-1, keepdims=True))
    return center * lax.rsqrt(spread + 1e-05)

def reference(tokens, query_weight, key_weight, value_weight, gate_weight, out_weight, log_decay):

    def one_sequence(inputs):
        token_rows, decay_rows = inputs
        positions = jnp.arange(SEQUENCE_LENGTH).astype(jnp.float32)

        def project(weight):
            return jnp.dot(token_rows, weight, preferred_element_type=jnp.float32)
        queries = rotate(project(query_weight).reshape(SEQUENCE_LENGTH, RETENTION_HEADS, DH), positions).astype(jnp.bfloat16)
        keys_all = rotate(project(key_weight).reshape(SEQUENCE_LENGTH, RETENTION_HEADS, DH), positions).astype(jnp.bfloat16)
        values_all = project(value_weight).reshape(SEQUENCE_LENGTH, RETENTION_HEADS, DH).astype(jnp.bfloat16)
        gate_values = project(gate_weight).astype(jnp.bfloat16)
        blocks = SEQUENCE_LENGTH // BLOCK
        causal = jnp.arange(BLOCK)[:, None] >= jnp.arange(BLOCK)[None, :]

        def advance(carried, block_data):
            q_block, k_block, v_block, d_block = block_data
            cumulative = jnp.cumsum(d_block, axis=0)
            scores = jnp.einsum('thd,shd->hts', q_block.astype(jnp.float32), k_block.astype(jnp.float32))
            leading = cumulative.T
            differ = leading[:, :, None] - leading[:, None, :]
            weights = jnp.where(causal, jnp.exp(jnp.where(causal, differ, 0.0)), 0.0)
            mixed_weights = (scores * weights).astype(jnp.bfloat16)
            intra_part = jnp.einsum('hts,shd->thd', mixed_weights.astype(jnp.float32), v_block.astype(jnp.float32))
            inter_part = jnp.exp(cumulative)[:, :, None] * jnp.einsum('thd,hde->the', q_block.astype(jnp.float32), carried, precision=lax.Precision.HIGHEST)
            ending = cumulative[-1]
            weighted = k_block.astype(jnp.float32) * jnp.exp(ending[None, :] - cumulative)[:, :, None]
            update = jnp.einsum('shd,she->hde', weighted, v_block.astype(jnp.float32), precision=lax.Precision.HIGHEST)
            return (jnp.exp(ending)[:, None, None] * carried + update, intra_part + inter_part)
        final_state, retained = lax.scan(advance, jnp.zeros((RETENTION_HEADS, DH, DH), jnp.float32), (queries.reshape(blocks, BLOCK, RETENTION_HEADS, DH), keys_all.reshape(blocks, BLOCK, RETENTION_HEADS, DH), values_all.reshape(blocks, BLOCK, RETENTION_HEADS, DH), decay_rows.reshape(blocks, BLOCK, RETENTION_HEADS)))
        normed = group_norm(retained.reshape(SEQUENCE_LENGTH, RETENTION_HEADS, DH)).reshape(SEQUENCE_LENGTH, D)
        hidden = (jax.nn.silu(gate_values.astype(jnp.float32)) * normed).astype(jnp.bfloat16)
        return jnp.dot(hidden, out_weight, preferred_element_type=jnp.float32).astype(jnp.bfloat16)
    return lax.map(one_sequence, (tokens, log_decay))
```

```python
import jax
import jax.numpy as jnp
import numpy as np
from jax import lax
from jax.experimental import pallas as pl
from jax.experimental.pallas import tpu as pltpu
from jax.sharding import PartitionSpec as P

DH = 256
HALF = DH // 2
BLOCK = 512
KEY, VALUE, QUERY, GATE = range(4)
F32, BF16 = jnp.float32, jnp.bfloat16


def dot(a, b):
    return jnp.dot(a, b, preferred_element_type=F32)


def rotation_rows(ctx_count, rows):
    frequency = 10000.0 ** (-np.arange(HALF) / HALF)
    tables = []
    for stride, count in ((32, rows // 32), (1, 32), (rows, ctx_count)):
        angles = (np.arange(count) * stride)[:, None] * frequency[None, :]
        tables += [np.cos(angles), np.sin(angles)]
    return [t.astype(np.float32) for t in tables]


def make_kernel(n_ctx, n_tp):
    n_peers = n_ctx - 1

    def kernel(
        tok, wk, wv, wq, wg, wo, ld, cos_a, sin_a, cos_b, sin_b, cos_c, sin_c, out,
        tokv, wown, woth, wov, acc, kb, vb, qb, gb, ret, ust, ubuf, rbuf, pbuf, sbuf,
        abuf, arcv, crow, ccol, cosv, sinv, hid, oacc, obuf,
        tsem, lsem, wsend, wrecv, asend, arecv, usend, urecv, psend, precv,
        wolocal, wosend, worecv, wofwd, agsend, agrecv, fwsend, fwrecv, osem,
    ):
        ctx, tp, core = (lax.axis_index(n) for n in ("ctx", "tp", "fsdp"))
        rows = tok.shape[0]
        khalf = tok.shape[1] // 2
        partner = {"fsdp": 1 - core}
        right = {"tp": lax.rem(tp + 1, n_tp)}
        left = {"tp": lax.rem(tp + n_tp - 1, n_tp)}
        weights = (wk, wv, wq, wg)

        barrier = pltpu.get_barrier_semaphore()
        pl.semaphore_signal(barrier, inc=1, device_id=partner)
        for k in range(1, n_tp):
            pl.semaphore_signal(barrier, inc=1, device_id={"tp": lax.rem(tp + k, n_tp)})

        def greet(k, carry):
            pl.semaphore_signal(barrier, inc=1, device_id={"ctx": lax.rem(ctx + k, n_ctx)})
            return carry

        lax.fori_loop(1, n_ctx, greet, 0)

        def tok_copy(part):
            half = core if part == 0 else 1 - core
            columns = pl.ds(pl.multiple_of(half * khalf, khalf), khalf)
            return pltpu.make_async_copy(tok.at[:, columns], tokv.at[part], tsem.at[part])

        def own_copy(i, h):
            source = weights[i].at[:, h * DH : (h + 1) * DH]
            return pltpu.make_async_copy(source, wown.at[i, h], lsem.at[i, h])

        order = [(KEY, 0), (VALUE, 0), (KEY, 1), (VALUE, 1), (QUERY, 0), (GATE, 0), (QUERY, 1), (GATE, 1)]
        tok_copy(0).start()
        for i, h in order[:2]:
            own_copy(i, h).start()
        tok_copy(1).start()
        for i, h in order[2:]:
            own_copy(i, h).start()

        crow[...] = jnp.zeros_like(crow)
        crow[0 : ld.shape[0], :] = ld[...]
        running = crow[...]
        lane = lax.rem(lax.broadcasted_iota(jnp.int32, running.shape, 1), BLOCK)
        step = 1
        while step < BLOCK:
            running = running + jnp.where(lane >= step, pltpu.roll(running, step, 1), 0.0)
            step *= 2
        crow[...] = running
        ccol[...] = running.T
        ends = [crow[:, (b + 1) * BLOCK - 1 : (b + 1) * BLOCK] for b in range(2)]
        total = ends[0] + ends[1]
        abuf[...] = jnp.broadcast_to(total, abuf.shape)
        arcv[ctx] = jnp.broadcast_to(total, abuf.shape)

        cc, sc = cos_c[pl.ds(ctx, 1), :], sin_c[pl.ds(ctx, 1), :]
        cosv[0:32, :] = cos_a[...] * cc - sin_a[...] * sc
        sinv[0:32, :] = sin_a[...] * cc + cos_a[...] * sc
        base_cos, base_sin = cosv[0:32, :], sinv[0:32, :]
        for a in range(rows // 32):
            ca, sa = base_cos[a : a + 1, :], base_sin[a : a + 1, :]
            cosv[a * 32 : (a + 1) * 32, :] = ca * cos_b[...] - sa * sin_b[...]
            sinv[a * 32 : (a + 1) * 32, :] = sa * cos_b[...] + ca * sin_b[...]

        def own_product(i, h):
            own_copy(i, h).wait()
            acc[i, h] = dot(tokv[0], wown[i, h])

        tok_copy(0).wait()
        own_product(KEY, 0)
        own_product(VALUE, 0)

        pl.semaphore_wait(barrier, 1 + (n_tp - 1) + n_peers)

        def swap(i, h):
            return pltpu.make_async_remote_copy(
                src_ref=weights[i].at[:, h * DH : (h + 1) * DH],
                dst_ref=woth.at[i, h],
                send_sem=wsend.at[i, h],
                recv_sem=wrecv.at[i, h],
                device_id=partner,
            )

        for i, h in order:
            swap(i, h).start()

        def send_total(k, carry):
            pltpu.make_async_remote_copy(
                src_ref=abuf,
                dst_ref=arcv.at[ctx],
                send_sem=asend,
                recv_sem=arecv,
                device_id={"ctx": lax.rem(ctx + k, n_ctx)},
            ).start()
            return carry

        lax.fori_loop(1, n_ctx, send_total, 0)

        per_core = n_tp // 2
        width = wo.shape[1] // per_core

        def wo_send(j):
            return pltpu.make_async_remote_copy(
                src_ref=wo.at[:, j * width : (j + 1) * width],
                dst_ref=wov.at[tp],
                send_sem=wosend.at[j],
                recv_sem=worecv.at[tp],
                device_id={"tp": per_core * core + j},
            )

        def wo_own(j):
            return pltpu.make_async_copy(
                wo.at[:, j * width : (j + 1) * width], wov.at[tp], wolocal
            )

        def wo_from(r):
            return pltpu.make_async_remote_copy(
                src_ref=wov.at[r],
                dst_ref=wov.at[r],
                send_sem=wofwd.at[r],
                recv_sem=worecv.at[r],
                device_id=partner,
            )

        for j in range(per_core):
            here = per_core * core + j == tp

            @pl.when(jnp.logical_not(here))
            def _():
                wo_send(j).start()

            @pl.when(here)
            def _():
                wo_own(j).start()

        def positions(b):
            return slice(b * BLOCK, (b + 1) * BLOCK)

        def project(i, h):
            swap(i, h).wait_recv()
            return acc[i, h] + dot(tokv[1], woth[i, h])

        def rotated(u):
            first, second = u[:, :HALF], u[:, HALF:]
            cosine, sine = cosv[...], sinv[...]
            return (first * cosine - second * sine).astype(BF16), (
                second * cosine + first * sine
            ).astype(BF16)

        def key_value(h):
            kb[h, :, :HALF], kb[h, :, HALF:] = rotated(project(KEY, h))
            vb[h] = project(VALUE, h).astype(BF16)

        def query_gate(h):
            qb[h, :, :HALF], qb[h, :, HALF:] = rotated(project(QUERY, h))
            gb[h] = project(GATE, h).astype(BF16)

        def block_end(h, b):
            return crow[h : h + 1, (b + 1) * BLOCK - 1 : (b + 1) * BLOCK]

        def decay_column(h, b):
            return ccol[positions(b), h : h + 1]

        def states(h):
            for b in range(2):
                scale = jnp.exp(block_end(h, b) - decay_column(h, b))
                scaled = (kb[h, positions(b)].astype(F32) * scale).astype(BF16)
                ust[h, b] = lax.dot_general(
                    scaled, vb[h, positions(b)], (((0,), (0,)), ((), ())),
                    preferred_element_type=F32,
                )
            joined = (jnp.exp(block_end(h, 1)) * ust[h, 0] + ust[h, 1]).astype(BF16)
            for j in range(2):
                ubuf[h, j * 16 : (j + 1) * 16] = joined[:, j * HALF : (j + 1) * HALF].reshape(16, 16, HALF)
            rbuf[h, ctx] = ubuf[h, ctx]

            def send(k, carry):
                to = lax.rem(ctx + k, n_ctx)
                pltpu.make_async_remote_copy(
                    src_ref=ubuf.at[h, to],
                    dst_ref=rbuf.at[h, ctx],
                    send_sem=usend.at[h],
                    recv_sem=urecv.at[h],
                    device_id={"ctx": to},
                ).start()
                return carry

            lax.fori_loop(1, n_ctx, send, 0)

        def many(buffer, send_sem, recv_sem):
            part = buffer.at[pl.ds(0, n_peers)]
            return pltpu.make_async_remote_copy(
                src_ref=part, dst_ref=part, send_sem=send_sem, recv_sem=recv_sem,
                device_id={"ctx": lax.rem(ctx + 1, n_ctx)},
            )

        def scan(h):
            many(rbuf.at[h], usend.at[h], urecv.at[h]).wait_recv()

            def hop(d, before):
                pbuf[h, d] = before.astype(BF16)
                return before * jnp.exp(arcv[d, h : h + 1, :]) + rbuf[h, d].astype(F32)

            lax.fori_loop(0, n_ctx, hop, jnp.zeros((16, HALF), F32))
            sbuf[h, ctx] = pbuf[h, ctx]

            def send(k, carry):
                to = lax.rem(ctx + k, n_ctx)
                pltpu.make_async_remote_copy(
                    src_ref=pbuf.at[h, to],
                    dst_ref=sbuf.at[h, ctx],
                    send_sem=psend.at[h],
                    recv_sem=precv.at[h],
                    device_id={"ctx": to},
                ).start()
                return carry

            lax.fori_loop(1, n_ctx, send, 0)

        quarter = BLOCK // 2

        def intra(h):
            for b in range(2):
                for part in range(2):
                    start = b * BLOCK + part * quarter
                    extent = (part + 1) * quarter
                    mine = slice(start, start + quarter)
                    seen = slice(b * BLOCK, b * BLOCK + extent)
                    scores = lax.dot_general(
                        qb[h, mine], kb[h, seen], (((1,), (1,)), ((), ())),
                        preferred_element_type=F32,
                    )
                    t = lax.broadcasted_iota(jnp.int32, scores.shape, 0) + part * quarter
                    s = lax.broadcasted_iota(jnp.int32, scores.shape, 1)
                    differ = ccol[mine, h : h + 1] - crow[h : h + 1, seen]
                    decay = jnp.exp(jnp.where(t >= s, differ, 0.0))
                    mixed = jnp.where(t >= s, scores * decay, 0.0).astype(BF16)
                    ret[h, mine] = dot(mixed, vb[h, seen])

        def ag_own(h, b, way):
            return pltpu.make_async_remote_copy(
                src_ref=hid.at[tp, h, b],
                dst_ref=hid.at[tp, h, b],
                send_sem=agsend.at[way, h, b],
                recv_sem=agrecv.at[way, h, b],
                device_id=right if way == 0 else left,
            )

        def ag_forward(h, way):
            source = lax.rem(tp + (n_tp - 1 if way == 0 else 1), n_tp)
            return pltpu.make_async_remote_copy(
                src_ref=hid.at[source, h, way],
                dst_ref=hid.at[source, h, way],
                send_sem=fwsend.at[way, h],
                recv_sem=fwrecv.at[way, h],
                device_id=right if way == 0 else left,
            )

        def finish(h):
            many(sbuf.at[h], psend.at[h], precv.at[h]).wait_recv()
            state = jnp.concatenate(
                [sbuf[h, j * 16 : (j + 1) * 16].reshape(DH, HALF) for j in range(2)], axis=1
            )
            later = (jnp.exp(block_end(h, 0)) * state.astype(F32) + ust[h, 0]).astype(BF16)
            for b in range(2):
                prior = state if b == 0 else later
                inter = jnp.exp(decay_column(h, b)) * dot(qb[h, positions(b)], prior)
                retained = ret[h, positions(b)] + inter
                center = retained - jnp.mean(retained, axis=-1, keepdims=True)
                spread = jnp.mean(center * center, axis=-1, keepdims=True)
                normed = center * lax.rsqrt(spread + 1e-5)
                gates = gb[h, positions(b)].astype(F32)
                silu = gates / (1.0 + jnp.exp(-gates))
                hid[tp, h, b] = (silu * normed).astype(BF16)
                for way in range(2):
                    ag_own(h, b, way).start()

        def fold(source, h, b, first=False):
            product = dot(hid[source, h, b], wov[source, h * DH : (h + 1) * DH, :])
            oacc[b] = product if first else oacc[b] + product

        for i, h in order[2:4]:
            own_product(i, h)
        tok_copy(1).wait()
        key_value(0)
        states(0)
        key_value(1)
        states(1)

        own_product(QUERY, 0)
        own_product(GATE, 0)
        query_gate(0)
        many(arcv, asend, arecv).wait_recv()
        scan(0)
        intra(0)
        own_product(QUERY, 1)
        own_product(GATE, 1)
        query_gate(1)
        scan(1)

        holder = tp // per_core == core
        for j in range(per_core):
            @pl.when(per_core * core + j == tp)
            def _():
                wo_own(j).wait()

        @pl.when(holder)
        def _():
            wo_from(tp).start()

        for k in range(1, n_tp):
            r = lax.rem(tp + k, n_tp)

            @pl.when(holder)
            def _():
                wo_from(r).wait_recv()
                wo_from(r).start()

        intra(1)
        finish(0)
        finish(1)

        @pl.when(jnp.logical_not(holder))
        def _():
            for r in range(n_tp):
                wo_from(r).wait_recv()

        @pl.when(holder)
        def _():
            for r in range(n_tp):
                wo_from(r).wait_send()

        for j in range(per_core):
            @pl.when(per_core * core + j != tp)
            def _():
                wo_send(j).wait_send()

        for h in range(2):
            for b in range(2):
                fold(tp, h, b, first=h == 0)
        before, after = lax.rem(tp + n_tp - 1, n_tp), lax.rem(tp + 1, n_tp)
        opposite = lax.rem(tp + 2, n_tp)
        for h in range(2):
            for b in range(2):
                ag_own(h, b, 0).wait_recv()
                if b == 0:
                    ag_forward(h, 0).start()
                ag_own(h, b, 1).wait_recv()
                if b == 1:
                    ag_forward(h, 1).start()
                fold(before, h, b)
                fold(after, h, b)
        for h in range(2):
            for way in range(2):
                ag_forward(h, way).wait_recv()
                fold(opposite, h, way)
                if h == 1:
                    obuf[positions(way)] = oacc[way].astype(BF16)
                    pltpu.make_async_copy(
                        obuf.at[positions(way)], out.at[positions(way)], osem.at[way]
                    ).start()

        for i, h in order:
            swap(i, h).wait_send()
        many(arcv, asend, arecv).wait_send()
        for h in range(2):
            many(rbuf.at[h], usend.at[h], urecv.at[h]).wait_send()
            many(sbuf.at[h], psend.at[h], precv.at[h]).wait_send()
            for way in range(2):
                for b in range(2):
                    ag_own(h, b, way).wait_send()
                ag_forward(h, way).wait_send()
        for way in range(2):
            pltpu.make_async_copy(
                obuf.at[positions(way)], out.at[positions(way)], osem.at[way]
            ).wait()

    return kernel


def solution(mesh):
    n_ctx, n_tp = mesh.shape["ctx"], mesh.shape["tp"]

    def on_device(tokens, query_weight, key_weight, value_weight, gate_weight, out_weight, log_decay):
        rows, depth = tokens.shape[1:]
        cols = query_weight.shape[1]
        out_rows = out_weight.shape[0]
        tables = rotation_rows(n_ctx, rows)
        vmem = lambda *shape, dtype=BF16: pltpu.VMEM(shape, dtype)
        dma = lambda *shape: pltpu.SemaphoreType.DMA(shape)
        anywhere = pl.BlockSpec(memory_space=pl.ANY)
        small = pl.BlockSpec(memory_space=pltpu.VMEM)
        result = pl.pallas_call(
            make_kernel(n_ctx, n_tp),
            out_shape=jax.ShapeDtypeStruct((rows, cols), BF16),
            in_specs=[anywhere] * 6 + [small] * 7,
            out_specs=anywhere,
            scratch_shapes=[
                vmem(2, rows, depth // 2),
                vmem(4, 2, depth // 2, DH),
                vmem(4, 2, depth // 2, DH),
                vmem(n_tp, out_rows, cols),
                vmem(4, 2, rows, DH, dtype=F32),
                vmem(2, rows, DH),
                vmem(2, rows, DH),
                vmem(2, rows, DH),
                vmem(2, rows, DH),
                vmem(2, rows, DH, dtype=F32),
                vmem(2, 2, DH, DH, dtype=F32),
                vmem(2, n_ctx, 16, HALF),
                vmem(2, n_ctx, 16, HALF),
                vmem(2, n_ctx, 16, HALF),
                vmem(2, n_ctx, 16, HALF),
                vmem(8, HALF, dtype=F32),
                vmem(n_ctx, 8, HALF, dtype=F32),
                vmem(8, rows, dtype=F32),
                vmem(rows, 8, dtype=F32),
                vmem(rows, HALF, dtype=F32),
                vmem(rows, HALF, dtype=F32),
                vmem(n_tp, 2, 2, BLOCK, DH),
                vmem(2, BLOCK, cols, dtype=F32),
                vmem(rows, cols),
                dma(2), dma(4, 2), dma(4, 2), dma(4, 2), dma(), dma(),
                dma(2), dma(2), dma(2), dma(2),
                dma(), dma(2), dma(n_tp), dma(n_tp),
                dma(2, 2, 2), dma(2, 2, 2), dma(2, 2), dma(2, 2), dma(2),
            ],
            compiler_params=pltpu.CompilerParams(
                collective_id=0, has_side_effects=True, vmem_limit_bytes=60 << 20
            ),
            name="retention",
        )(
            tokens[0], key_weight, value_weight, query_weight, gate_weight, out_weight,
            jnp.transpose(log_decay[0]), *tables,
        )
        return result[None]

    in_specs = (
        P("fsdp", "ctx", None),
        P("fsdp", "tp"),
        P("fsdp", "tp"),
        P("fsdp", "tp"),
        P("fsdp", "tp"),
        P("tp", "fsdp"),
        P("fsdp", "ctx", "tp"),
    )
    out_specs = P("fsdp", "ctx", "tp")
    return jax.shard_map(
        on_device, mesh=mesh, in_specs=in_specs, out_specs=out_specs, check_vma=False
    )
```

```python
import jax
import jax.numpy as jnp
import numpy as np
from jax import lax
from jax.experimental import pallas as pl
from jax.experimental.pallas import tpu as pltpu
from jax.sharding import PartitionSpec as P

DH = 256
HALF = DH // 2
BLOCK = 512
KEY, VALUE, QUERY, GATE = range(4)
F32, BF16 = jnp.float32, jnp.bfloat16


def dot(a, b):
    return jnp.dot(a, b, preferred_element_type=F32)


def rotation_rows(ctx_count, rows):
    frequency = 10000.0 ** (-np.arange(HALF) / HALF)
    tables = []
    for stride, count in ((32, rows // 32), (1, 32), (rows, ctx_count)):
        angles = (np.arange(count) * stride)[:, None] * frequency[None, :]
        tables += [np.cos(angles), np.sin(angles)]
    return [t.astype(np.float32) for t in tables]


def make_kernel(n_ctx, n_tp):
    n_peers = n_ctx - 1

    def kernel(
        tok, wk, wv, wq, wg, wo, ld, cos_a, sin_a, cos_b, sin_b, cos_c, sin_c, out,
        tokv, wv_all, wov, acc, kb, vb, qb, gb, ret, ust, ubuf, rbuf, pbuf, sbuf,
        abuf, arcv, crow, ccol, cosv, sinv, hid, oacc, obuf,
        tsem, lsem, wsend, wrecv, asend, arecv, usend, urecv, psend, precv,
        wolocal, wosend, worecv, wofwd, agsend, agrecv, fwsend, fwrecv, osem,
    ):
        ctx, tp, core = (lax.axis_index(n) for n in ("ctx", "tp", "fsdp"))
        rows = tok.shape[0]
        khalf = tok.shape[1] // 2
        partner = {"fsdp": 1 - core}
        right = {"tp": lax.rem(tp + 1, n_tp)}
        left = {"tp": lax.rem(tp + n_tp - 1, n_tp)}
        weights = (wk, wv, wq, wg)

        barrier = pltpu.get_barrier_semaphore()
        pl.semaphore_signal(barrier, inc=1, device_id=partner)
        for k in range(1, n_tp):
            pl.semaphore_signal(barrier, inc=1, device_id={"tp": lax.rem(tp + k, n_tp)})

        def greet(k, carry):
            pl.semaphore_signal(barrier, inc=1, device_id={"ctx": lax.rem(ctx + k, n_ctx)})
            return carry

        lax.fori_loop(1, n_ctx, greet, 0)

        own_rows = pl.ds(pl.multiple_of(core * khalf, khalf), khalf)
        other_rows = pl.ds(pl.multiple_of((1 - core) * khalf, khalf), khalf)

        def tok_copy(part):
            columns = own_rows if part == 0 else other_rows
            return pltpu.make_async_copy(tok.at[:, columns], tokv.at[:, columns], tsem.at[part])

        def own_copy(i, h):
            source = weights[i].at[:, h * DH : (h + 1) * DH]
            return pltpu.make_async_copy(source, wv_all.at[i, h, own_rows], lsem.at[i, h])

        order = [(KEY, 0), (VALUE, 0), (QUERY, 0), (GATE, 0), (KEY, 1), (VALUE, 1), (QUERY, 1), (GATE, 1)]
        tok_copy(0).start()
        for i, h in order[:2]:
            own_copy(i, h).start()
        tok_copy(1).start()
        for i, h in order[2:]:
            own_copy(i, h).start()

        crow[...] = jnp.zeros_like(crow)
        crow[0 : ld.shape[0], :] = ld[...]
        running = crow[...]
        lane = lax.rem(lax.broadcasted_iota(jnp.int32, running.shape, 1), BLOCK)
        step = 1
        while step < BLOCK:
            running = running + jnp.where(lane >= step, pltpu.roll(running, step, 1), 0.0)
            step *= 2
        crow[...] = running
        ccol[...] = running.T
        ends = [crow[:, (b + 1) * BLOCK - 1 : (b + 1) * BLOCK] for b in range(2)]
        total = ends[0] + ends[1]
        abuf[...] = jnp.broadcast_to(total, abuf.shape)
        arcv[ctx] = jnp.broadcast_to(total, abuf.shape)

        pl.semaphore_wait(barrier, 1 + (n_tp - 1) + n_peers)

        def swap(i, h):
            return pltpu.make_async_remote_copy(
                src_ref=weights[i].at[:, h * DH : (h + 1) * DH],
                dst_ref=wv_all.at[i, h, own_rows],
                send_sem=wsend.at[i, h],
                recv_sem=wrecv.at[i, h],
                device_id=partner,
            )

        for i, h in order:
            swap(i, h).start()

        def send_total(k, carry):
            pltpu.make_async_remote_copy(
                src_ref=abuf,
                dst_ref=arcv.at[ctx],
                send_sem=asend,
                recv_sem=arecv,
                device_id={"ctx": lax.rem(ctx + k, n_ctx)},
            ).start()
            return carry

        lax.fori_loop(1, n_ctx, send_total, 0)

        per_core = n_tp // 2
        width = wo.shape[1] // per_core

        def wo_send(j):
            return pltpu.make_async_remote_copy(
                src_ref=wo.at[:, j * width : (j + 1) * width],
                dst_ref=wov.at[tp],
                send_sem=wosend.at[j],
                recv_sem=worecv.at[tp],
                device_id={"tp": per_core * core + j},
            )

        def wo_own(j):
            return pltpu.make_async_copy(
                wo.at[:, j * width : (j + 1) * width], wov.at[tp], wolocal
            )

        def wo_from(r):
            return pltpu.make_async_remote_copy(
                src_ref=wov.at[r],
                dst_ref=wov.at[r],
                send_sem=wofwd.at[r],
                recv_sem=worecv.at[r],
                device_id=partner,
            )

        for j in range(per_core):
            here = per_core * core + j == tp

            @pl.when(jnp.logical_not(here))
            def _():
                wo_send(j).start()

            @pl.when(here)
            def _():
                wo_own(j).start()

        cc, sc = cos_c[pl.ds(ctx, 1), :], sin_c[pl.ds(ctx, 1), :]
        cosv[0:32, :] = cos_a[...] * cc - sin_a[...] * sc
        sinv[0:32, :] = sin_a[...] * cc + cos_a[...] * sc
        base_cos, base_sin = cosv[0:32, :], sinv[0:32, :]
        for a in range(rows // 32):
            ca, sa = base_cos[a : a + 1, :], base_sin[a : a + 1, :]
            cosv[a * 32 : (a + 1) * 32, :] = ca * cos_b[...] - sa * sin_b[...]
            sinv[a * 32 : (a + 1) * 32, :] = sa * cos_b[...] + ca * sin_b[...]

        def positions(b):
            return slice(b * BLOCK, (b + 1) * BLOCK)

        def own_product(i, h):
            own_copy(i, h).wait()
            acc[i] = dot(tokv[:, own_rows], wv_all[i, h, own_rows])

        def project(i, h, split=False):
            if split:
                swap(i, h).wait_recv()
                return acc[i] + dot(tokv[:, other_rows], wv_all[i, h, other_rows])
            own_copy(i, h).wait()
            swap(i, h).wait_recv()
            return dot(tokv[...], wv_all[i, h])

        def rotated(u):
            first, second = u[:, :HALF], u[:, HALF:]
            cosine, sine = cosv[...], sinv[...]
            return (first * cosine - second * sine).astype(BF16), (
                second * cosine + first * sine
            ).astype(BF16)

        def key_value(h):
            split = h == 0
            kb[h, :, :HALF], kb[h, :, HALF:] = rotated(project(KEY, h, split))
            vb[h] = project(VALUE, h, split).astype(BF16)

        def query_gate(h):
            qb[h, :, :HALF], qb[h, :, HALF:] = rotated(project(QUERY, h))
            gb[h] = project(GATE, h).astype(BF16)

        def block_end(h, b):
            return crow[h : h + 1, (b + 1) * BLOCK - 1 : (b + 1) * BLOCK]

        def decay_column(h, b):
            return ccol[positions(b), h : h + 1]

        def states(h):
            for b in range(2):
                scale = jnp.exp(block_end(h, b) - decay_column(h, b))
                scaled = (kb[h, positions(b)].astype(F32) * scale).astype(BF16)
                ust[h, b] = lax.dot_general(
                    scaled, vb[h, positions(b)], (((0,), (0,)), ((), ())),
                    preferred_element_type=F32,
                )
            joined = (jnp.exp(block_end(h, 1)) * ust[h, 0] + ust[h, 1]).astype(BF16)
            for j in range(2):
                ubuf[h, j * 16 : (j + 1) * 16] = joined[:, j * HALF : (j + 1) * HALF].reshape(16, 16, HALF)
            rbuf[h, ctx] = ubuf[h, ctx]

            def send(k, carry):
                to = lax.rem(ctx + k, n_ctx)
                pltpu.make_async_remote_copy(
                    src_ref=ubuf.at[h, to],
                    dst_ref=rbuf.at[h, ctx],
                    send_sem=usend.at[h],
                    recv_sem=urecv.at[h],
                    device_id={"ctx": to},
                ).start()
                return carry

            lax.fori_loop(1, n_ctx, send, 0)

        def many(buffer, send_sem, recv_sem):
            part = buffer.at[pl.ds(0, n_peers)]
            return pltpu.make_async_remote_copy(
                src_ref=part, dst_ref=part, send_sem=send_sem, recv_sem=recv_sem,
                device_id={"ctx": lax.rem(ctx + 1, n_ctx)},
            )

        def scan(h):
            many(rbuf.at[h], usend.at[h], urecv.at[h]).wait_recv()

            def hop(d, before):
                pbuf[h, d] = before.astype(BF16)
                return before * jnp.exp(arcv[d, h : h + 1, :]) + rbuf[h, d].astype(F32)

            lax.fori_loop(0, n_ctx, hop, jnp.zeros((16, HALF), F32))
            sbuf[h, ctx] = pbuf[h, ctx]

            def send(k, carry):
                to = lax.rem(ctx + k, n_ctx)
                pltpu.make_async_remote_copy(
                    src_ref=pbuf.at[h, to],
                    dst_ref=sbuf.at[h, ctx],
                    send_sem=psend.at[h],
                    recv_sem=precv.at[h],
                    device_id={"ctx": to},
                ).start()
                return carry

            lax.fori_loop(1, n_ctx, send, 0)

        quarter = BLOCK // 2

        def intra(h):
            for b in range(2):
                for part in range(2):
                    start = b * BLOCK + part * quarter
                    extent = (part + 1) * quarter
                    mine = slice(start, start + quarter)
                    seen = slice(b * BLOCK, b * BLOCK + extent)
                    scores = lax.dot_general(
                        qb[h, mine], kb[h, seen], (((1,), (1,)), ((), ())),
                        preferred_element_type=F32,
                    )
                    t = lax.broadcasted_iota(jnp.int32, scores.shape, 0) + part * quarter
                    s = lax.broadcasted_iota(jnp.int32, scores.shape, 1)
                    differ = ccol[mine, h : h + 1] - crow[h : h + 1, seen]
                    decay = jnp.exp(jnp.where(t >= s, differ, 0.0))
                    mixed = jnp.where(t >= s, scores * decay, 0.0).astype(BF16)
                    ret[h, mine] = dot(mixed, vb[h, seen])

        def ag_own(h, b, way):
            return pltpu.make_async_remote_copy(
                src_ref=hid.at[tp, h, b],
                dst_ref=hid.at[tp, h, b],
                send_sem=agsend.at[way, h, b],
                recv_sem=agrecv.at[way, h, b],
                device_id=right if way == 0 else left,
            )

        def ag_forward(h, way):
            source = lax.rem(tp + (n_tp - 1 if way == 0 else 1), n_tp)
            return pltpu.make_async_remote_copy(
                src_ref=hid.at[source, h, way],
                dst_ref=hid.at[source, h, way],
                send_sem=fwsend.at[way, h],
                recv_sem=fwrecv.at[way, h],
                device_id=right if way == 0 else left,
            )

        def finish(h):
            many(sbuf.at[h], psend.at[h], precv.at[h]).wait_recv()
            state = jnp.concatenate(
                [sbuf[h, j * 16 : (j + 1) * 16].reshape(DH, HALF) for j in range(2)], axis=1
            )
            later = (jnp.exp(block_end(h, 0)) * state.astype(F32) + ust[h, 0]).astype(BF16)
            for b in range(2):
                prior = state if b == 0 else later
                inter = jnp.exp(decay_column(h, b)) * dot(qb[h, positions(b)], prior)
                retained = ret[h, positions(b)] + inter
                center = retained - jnp.mean(retained, axis=-1, keepdims=True)
                spread = jnp.mean(center * center, axis=-1, keepdims=True)
                normed = center * lax.rsqrt(spread + 1e-5)
                gates = gb[h, positions(b)].astype(F32)
                silu = gates / (1.0 + jnp.exp(-gates))
                hid[tp, h, b] = (silu * normed).astype(BF16)
                ag_own(h, b, b).start()
            ag_own(h, 1, 0).start()
            ag_own(h, 0, 1).start()

        def fold(source, h, b, first=False):
            product = dot(hid[source, h, b], wov[source, h * DH : (h + 1) * DH, :])
            oacc[b] = product if first else oacc[b] + product

        tok_copy(0).wait()
        own_product(KEY, 0)
        own_product(VALUE, 0)
        tok_copy(1).wait()
        key_value(0)
        states(0)
        query_gate(0)
        intra(0)
        many(arcv, asend, arecv).wait_recv()
        scan(0)
        key_value(1)
        states(1)
        query_gate(1)
        finish(0)

        holder = tp // per_core == core
        for j in range(per_core):
            @pl.when(per_core * core + j == tp)
            def _():
                wo_own(j).wait()

        @pl.when(holder)
        def _():
            wo_from(tp).start()

        for k in range(1, n_tp):
            r = lax.rem(tp + k, n_tp)

            @pl.when(holder)
            def _():
                wo_from(r).wait_recv()
                wo_from(r).start()

        intra(1)
        scan(1)

        @pl.when(jnp.logical_not(holder))
        def _():
            for r in range(n_tp):
                wo_from(r).wait_recv()

        before, after = lax.rem(tp + n_tp - 1, n_tp), lax.rem(tp + 1, n_tp)
        opposite = lax.rem(tp + 2, n_tp)

        def neighbours(h):
            for way in range(2):
                ag_own(h, way, way).wait_recv()
                ag_forward(h, way).start()
            fold(before, h, 0)
            fold(after, h, 1)

        for b in range(2):
            fold(tp, 0, b, first=True)
        neighbours(0)
        finish(1)
        for b in range(2):
            fold(tp, 1, b)
        for h in range(2):
            if h == 1:
                neighbours(h)
            ag_own(h, 1, 0).wait_recv()
            fold(before, h, 1)
            ag_own(h, 0, 1).wait_recv()
            fold(after, h, 0)
            for way in range(2):
                ag_forward(h, way).wait_recv()
                fold(opposite, h, way)
                if h == 1:
                    obuf[positions(way)] = oacc[way].astype(BF16)
                    pltpu.make_async_copy(
                        obuf.at[positions(way)], out.at[positions(way)], osem.at[way]
                    ).start()

        @pl.when(holder)
        def _():
            for r in range(n_tp):
                wo_from(r).wait_send()

        for j in range(per_core):
            @pl.when(per_core * core + j != tp)
            def _():
                wo_send(j).wait_send()

        for i, h in order:
            swap(i, h).wait_send()
        many(arcv, asend, arecv).wait_send()
        for h in range(2):
            many(rbuf.at[h], usend.at[h], urecv.at[h]).wait_send()
            many(sbuf.at[h], psend.at[h], precv.at[h]).wait_send()
            for way in range(2):
                for b in range(2):
                    ag_own(h, b, way).wait_send()
                ag_forward(h, way).wait_send()
        for way in range(2):
            pltpu.make_async_copy(
                obuf.at[positions(way)], out.at[positions(way)], osem.at[way]
            ).wait()

    return kernel


def solution(mesh):
    n_ctx, n_tp = mesh.shape["ctx"], mesh.shape["tp"]

    def on_device(tokens, query_weight, key_weight, value_weight, gate_weight, out_weight, log_decay):
        rows, depth = tokens.shape[1:]
        cols = query_weight.shape[1]
        out_rows = out_weight.shape[0]
        tables = rotation_rows(n_ctx, rows)
        vmem = lambda *shape, dtype=BF16: pltpu.VMEM(shape, dtype)
        dma = lambda *shape: pltpu.SemaphoreType.DMA(shape)
        anywhere = pl.BlockSpec(memory_space=pl.ANY)
        small = pl.BlockSpec(memory_space=pltpu.VMEM)
        result = pl.pallas_call(
            make_kernel(n_ctx, n_tp),
            out_shape=jax.ShapeDtypeStruct((rows, cols), BF16),
            in_specs=[anywhere] * 6 + [small] * 7,
            out_specs=anywhere,
            scratch_shapes=[
                vmem(rows, depth),
                vmem(4, 2, depth, DH),
                vmem(n_tp, out_rows, cols),
                vmem(2, rows, DH, dtype=F32),
                vmem(2, rows, DH),
                vmem(2, rows, DH),
                vmem(2, rows, DH),
                vmem(2, rows, DH),
                vmem(2, rows, DH, dtype=F32),
                vmem(2, 2, DH, DH, dtype=F32),
                vmem(2, n_ctx, 16, HALF),
                vmem(2, n_ctx, 16, HALF),
                vmem(2, n_ctx, 16, HALF),
                vmem(2, n_ctx, 16, HALF),
                vmem(8, HALF, dtype=F32),
                vmem(n_ctx, 8, HALF, dtype=F32),
                vmem(8, rows, dtype=F32),
                vmem(rows, 8, dtype=F32),
                vmem(rows, HALF, dtype=F32),
                vmem(rows, HALF, dtype=F32),
                vmem(n_tp, 2, 2, BLOCK, DH),
                vmem(2, BLOCK, cols, dtype=F32),
                vmem(rows, cols),
                dma(2), dma(4, 2), dma(4, 2), dma(4, 2), dma(), dma(),
                dma(2), dma(2), dma(2), dma(2),
                dma(), dma(2), dma(n_tp), dma(n_tp),
                dma(2, 2, 2), dma(2, 2, 2), dma(2, 2), dma(2, 2), dma(2),
            ],
            compiler_params=pltpu.CompilerParams(
                collective_id=0, has_side_effects=True, vmem_limit_bytes=60 << 20
            ),
            name="retention",
        )(
            tokens[0], key_weight, value_weight, query_weight, gate_weight, out_weight,
            jnp.transpose(log_decay[0]), *tables,
        )
        return result[None]

    in_specs = (
        P("fsdp", "ctx", None),
        P("fsdp", "tp"),
        P("fsdp", "tp"),
        P("fsdp", "tp"),
        P("fsdp", "tp"),
        P("tp", "fsdp"),
        P("fsdp", "ctx", "tp"),
    )
    out_specs = P("fsdp", "ctx", "tp")
    return jax.shard_map(
        on_device, mesh=mesh, in_specs=in_specs, out_specs=out_specs, check_vma=False
    )
```

```python
import jax
import jax.numpy as jnp
import numpy as np
from jax import lax
from jax.experimental import pallas as pl
from jax.experimental.pallas import tpu as pltpu
from jax.sharding import PartitionSpec as P

DH = 256
HALF = DH // 2
BLOCK = 512
PIECES = 4
PIECE = BLOCK // PIECES
KEY, VALUE, QUERY, GATE = range(4)
F32, BF16 = jnp.float32, jnp.bfloat16


def dot(a, b):
    return jnp.dot(a, b, preferred_element_type=F32)


def rotation_rows(ctx_count, rows):
    frequency = 10000.0 ** (-np.arange(HALF) / HALF)
    tables = []
    for stride, count in ((32, rows // 32), (1, 32), (rows, ctx_count)):
        angles = (np.arange(count) * stride)[:, None] * frequency[None, :]
        tables += [np.cos(angles), np.sin(angles)]
    return [t.astype(np.float32) for t in tables]


def make_kernel(n_ctx, n_tp):
    n_peers = n_ctx - 1

    def kernel(
        tok, wk, wv, wq, wg, wo, ld, cos_a, sin_a, cos_b, sin_b, cos_c, sin_c, out,
        tokv, wv_all, wov, acc, kb, vb, qb, gb, ret, ust, ubuf, rbuf, pbuf, sbuf,
        abuf, arcv, crow, ccol, cosv, sinv, stv, hid, away, oacc, obuf,
        tsem, lsem, wsend, wrecv, asend, arecv, usend, urecv, psend, precv,
        wolocal, wosend, worecv, wofwd, wogot, crsend, crrecv, mtsend, mtrecv,
        fwsend, fwrecv, p2send, p2recv, osem,
    ):
        ctx, tp, core = (lax.axis_index(n) for n in ("ctx", "tp", "fsdp"))
        rows = tok.shape[0]
        khalf = tok.shape[1] // 2
        partner = {"fsdp": 1 - core}
        mate_tp, cross_tp = tp + 1 - 2 * lax.rem(tp, 2), n_tp - 1 - tp
        opposite_tp = lax.rem(tp + 2, n_tp)
        mate, cross = {"tp": mate_tp}, {"tp": cross_tp}
        mine = tp // 2
        weights = (wk, wv, wq, wg)

        barrier = pltpu.get_barrier_semaphore()
        pl.semaphore_signal(barrier, inc=1, device_id=partner)
        pl.semaphore_signal(barrier, inc=1, device_id=mate)
        pl.semaphore_signal(barrier, inc=1, device_id=cross)

        def greet(k, carry):
            pl.semaphore_signal(barrier, inc=1, device_id={"ctx": lax.rem(ctx + k, n_ctx)})
            return carry

        lax.fori_loop(1, n_ctx, greet, 0)

        own_rows = pl.ds(pl.multiple_of(core * khalf, khalf), khalf)
        other_rows = pl.ds(pl.multiple_of((1 - core) * khalf, khalf), khalf)

        def tok_copy(part):
            columns = own_rows if part == 0 else other_rows
            return pltpu.make_async_copy(tok.at[:, columns], tokv.at[:, columns], tsem.at[part])

        def own_copy(i, h):
            source = weights[i].at[:, h * DH : (h + 1) * DH]
            return pltpu.make_async_copy(source, wv_all.at[i, h, own_rows], lsem.at[i, h])

        order = [(KEY, 0), (VALUE, 0), (QUERY, 0), (GATE, 0), (KEY, 1), (VALUE, 1), (QUERY, 1), (GATE, 1)]
        tok_copy(0).start()
        for i, h in order[:2]:
            own_copy(i, h).start()
        tok_copy(1).start()
        for i, h in order[2:]:
            own_copy(i, h).start()

        crow[...] = jnp.zeros_like(crow)
        crow[0 : ld.shape[0], :] = ld[...]
        running = crow[...]
        lane = lax.rem(lax.broadcasted_iota(jnp.int32, running.shape, 1), BLOCK)
        step = 1
        while step < BLOCK:
            running = running + jnp.where(lane >= step, pltpu.roll(running, step, 1), 0.0)
            step *= 2
        crow[...] = running
        ccol[...] = running.T
        ends = [crow[:, (b + 1) * BLOCK - 1 : (b + 1) * BLOCK] for b in range(2)]
        total = ends[0] + ends[1]
        abuf[...] = jnp.broadcast_to(total, abuf.shape)
        arcv[ctx] = jnp.broadcast_to(total, abuf.shape)

        pl.semaphore_wait(barrier, 3 + n_peers)

        def swap(i, h):
            return pltpu.make_async_remote_copy(
                src_ref=weights[i].at[:, h * DH : (h + 1) * DH],
                dst_ref=wv_all.at[i, h, own_rows],
                send_sem=wsend.at[i, h],
                recv_sem=wrecv.at[i, h],
                device_id=partner,
            )

        for i, h in order:
            swap(i, h).start()

        def send_total(k, carry):
            pltpu.make_async_remote_copy(
                src_ref=abuf,
                dst_ref=arcv.at[ctx],
                send_sem=asend,
                recv_sem=arecv,
                device_id={"ctx": lax.rem(ctx + k, n_ctx)},
            ).start()
            return carry

        lax.fori_loop(1, n_ctx, send_total, 0)

        width = wo.shape[1] // 2
        group = lax.rem((tp + 1) // 2, 2)
        near = group + core * (1 - 2 * group)

        def wo_columns(index):
            return wo.at[:, pl.ds(pl.multiple_of(index * width, width), width)]

        def wo_own():
            return pltpu.make_async_copy(wo_columns(near), wov.at[core, tp], wolocal)

        def wo_copy(source, r, k, to):
            return pltpu.make_async_remote_copy(
                src_ref=source, dst_ref=wov.at[core, r], send_sem=wosend.at[k],
                recv_sem=worecv.at[k], device_id=to,
            )

        def wo_cross():
            return wo_copy(wo_columns(near), tp, 0, cross)

        def wo_mate():
            return wo_copy(wo_columns(1 - near), tp, 1, mate)

        def wo_relay():
            return wo_copy(wov.at[core, mate_tp], mate_tp, 2, cross)

        def wo_hand(r):
            return pltpu.make_async_remote_copy(
                src_ref=wov.at[core, r], dst_ref=wov.at[core, r], send_sem=wofwd.at[r],
                recv_sem=wogot.at[r], device_id=partner,
            )

        wo_own().start()
        wo_mate().start()
        wo_cross().start()

        cc, sc = cos_c[pl.ds(ctx, 1), :], sin_c[pl.ds(ctx, 1), :]
        cosv[0:32, :] = cos_a[...] * cc - sin_a[...] * sc
        sinv[0:32, :] = sin_a[...] * cc + cos_a[...] * sc
        base_cos, base_sin = cosv[0:32, :], sinv[0:32, :]
        for a in range(rows // 32):
            ca, sa = base_cos[a : a + 1, :], base_sin[a : a + 1, :]
            cosv[a * 32 : (a + 1) * 32, :] = ca * cos_b[...] - sa * sin_b[...]
            sinv[a * 32 : (a + 1) * 32, :] = sa * cos_b[...] + ca * sin_b[...]

        def positions(b):
            return slice(b * BLOCK, (b + 1) * BLOCK)

        def own_product(i, h):
            own_copy(i, h).wait()
            acc[i] = dot(tokv[:, own_rows], wv_all[i, h, own_rows])

        def project(i, h, split=False):
            if split:
                swap(i, h).wait_recv()
                return acc[i] + dot(tokv[:, other_rows], wv_all[i, h, other_rows])
            own_copy(i, h).wait()
            swap(i, h).wait_recv()
            return dot(tokv[...], wv_all[i, h])

        def rotated(u):
            first, second = u[:, :HALF], u[:, HALF:]
            cosine, sine = cosv[...], sinv[...]
            return (first * cosine - second * sine).astype(BF16), (
                second * cosine + first * sine
            ).astype(BF16)

        def key_value(h):
            split = h == 0
            kb[h, :, :HALF], kb[h, :, HALF:] = rotated(project(KEY, h, split))
            vb[h] = project(VALUE, h, split).astype(BF16)

        def query_gate(h):
            qb[h, :, :HALF], qb[h, :, HALF:] = rotated(project(QUERY, h))
            gb[h] = project(GATE, h).astype(BF16)

        def block_end(h, b):
            return crow[h : h + 1, (b + 1) * BLOCK - 1 : (b + 1) * BLOCK]

        def decay_column(h, b):
            return ccol[positions(b), h : h + 1]

        def states(h):
            for b in range(2):
                scale = jnp.exp(block_end(h, b) - decay_column(h, b))
                scaled = (kb[h, positions(b)].astype(F32) * scale).astype(BF16)
                ust[h, b] = lax.dot_general(
                    scaled, vb[h, positions(b)], (((0,), (0,)), ((), ())),
                    preferred_element_type=F32,
                )
            joined = (jnp.exp(block_end(h, 1)) * ust[h, 0] + ust[h, 1]).astype(BF16)
            for j in range(2):
                ubuf[h, j * 16 : (j + 1) * 16] = joined[:, j * HALF : (j + 1) * HALF].reshape(16, 16, HALF)
            rbuf[h, ctx] = ubuf[h, ctx]

            def send(k, carry):
                to = lax.rem(ctx + k, n_ctx)
                pltpu.make_async_remote_copy(
                    src_ref=ubuf.at[h, to],
                    dst_ref=rbuf.at[h, ctx],
                    send_sem=usend.at[h],
                    recv_sem=urecv.at[h],
                    device_id={"ctx": to},
                ).start()
                return carry

            lax.fori_loop(1, n_ctx, send, 0)

        def many(buffer, send_sem, recv_sem):
            part = buffer.at[pl.ds(0, n_peers)]
            return pltpu.make_async_remote_copy(
                src_ref=part, dst_ref=part, send_sem=send_sem, recv_sem=recv_sem,
                device_id={"ctx": lax.rem(ctx + 1, n_ctx)},
            )

        def scan(h):
            many(rbuf.at[h], usend.at[h], urecv.at[h]).wait_recv()

            def hop(d, before):
                pbuf[h, d] = before.astype(BF16)
                return before * jnp.exp(arcv[d, h : h + 1, :]) + rbuf[h, d].astype(F32)

            lax.fori_loop(0, n_ctx, hop, jnp.zeros((16, HALF), F32))
            sbuf[h, ctx] = pbuf[h, ctx]

            def send(k, carry):
                to = lax.rem(ctx + k, n_ctx)
                pltpu.make_async_remote_copy(
                    src_ref=pbuf.at[h, to],
                    dst_ref=sbuf.at[h, ctx],
                    send_sem=psend.at[h],
                    recv_sem=precv.at[h],
                    device_id={"ctx": to},
                ).start()
                return carry

            lax.fori_loop(1, n_ctx, send, 0)

        quarter = BLOCK // 2

        def intra(h):
            for b in range(2):
                for part in range(2):
                    start = b * BLOCK + part * quarter
                    extent = (part + 1) * quarter
                    mine = slice(start, start + quarter)
                    seen = slice(b * BLOCK, b * BLOCK + extent)
                    scores = lax.dot_general(
                        qb[h, mine], kb[h, seen], (((1,), (1,)), ((), ())),
                        preferred_element_type=F32,
                    )
                    t = lax.broadcasted_iota(jnp.int32, scores.shape, 0) + part * quarter
                    s = lax.broadcasted_iota(jnp.int32, scores.shape, 1)
                    differ = ccol[mine, h : h + 1] - crow[h : h + 1, seen]
                    decay = jnp.exp(jnp.where(t >= s, differ, 0.0))
                    mixed = jnp.where(t >= s, scores * decay, 0.0).astype(BF16)
                    ret[h, mine] = dot(mixed, vb[h, seen])

        def piece(p):
            return pl.ds(p * PIECE, PIECE)

        def hidden_copy(source, owner, h, p, sends, receives, to):
            return pltpu.make_async_remote_copy(
                src_ref=source, dst_ref=hid.at[owner, h, piece(p)], send_sem=sends.at[h, p],
                recv_sem=receives.at[h, p], device_id=to,
            )

        def to_cross(h, p):
            return hidden_copy(away.at[h, piece(p)], tp, h, p, crsend, crrecv, cross)

        def to_mate(h, p):
            return hidden_copy(hid.at[tp, h, piece(p)], tp, h, p, mtsend, mtrecv, mate)

        def forward(h, p):
            source = hid.at[cross_tp, h, piece(p)]
            return hidden_copy(source, cross_tp, h, p, fwsend, fwrecv, mate)

        def finish(h):
            many(sbuf.at[h], psend.at[h], precv.at[h]).wait_recv()
            state = jnp.concatenate(
                [sbuf[h, j * 16 : (j + 1) * 16].reshape(DH, HALF) for j in range(2)], axis=1
            )
            stv[0] = state
            stv[1] = (jnp.exp(block_end(h, 0)) * state.astype(F32) + ust[h, 0]).astype(BF16)

            def hidden(b):
                at = pl.ds(pl.multiple_of(b * BLOCK, BLOCK), BLOCK)
                inter = jnp.exp(ccol[at, h : h + 1]) * dot(qb[h, at], stv[b])
                retained = ret[h, at] + inter
                center = retained - jnp.mean(retained, axis=-1, keepdims=True)
                spread = jnp.mean(center * center, axis=-1, keepdims=True)
                normed = center * lax.rsqrt(spread + 1e-5)
                gates = gb[h, at].astype(F32)
                silu = gates / (1.0 + jnp.exp(-gates))
                return (silu * normed).astype(BF16)

            away[h] = hidden(1 - mine)
            for p in range(PIECES):
                to_cross(h, p).start()
            hid[tp, h] = hidden(mine)

        def fold(source, h, at=slice(None), first=False):
            for slot in range(2):
                product = dot(hid[source, h, at], wov[slot, source, h * DH : (h + 1) * DH, :])
                oacc[slot, at] = product if first else oacc[slot, at] + product

        tok_copy(0).wait()
        own_product(KEY, 0)
        own_product(VALUE, 0)
        tok_copy(1).wait()
        key_value(0)
        states(0)
        query_gate(0)
        intra(0)
        many(arcv, asend, arecv).wait_recv()
        wo_mate().wait_recv()
        wo_relay().start()
        scan(0)
        key_value(1)
        states(1)
        query_gate(1)
        finish(0)
        for p in range(PIECES):
            to_mate(0, p).start()

        wo_own().wait()
        wo_cross().wait_recv()
        for r in (tp, mate_tp, cross_tp):
            wo_hand(r).start()
        intra(1)
        scan(1)
        wo_relay().wait_recv()
        wo_hand(opposite_tp).start()
        for p in range(PIECES):
            to_cross(0, p).wait_recv()
            forward(0, p).start()
        for r in range(n_tp):
            wo_hand(r).wait_recv()
        fold(tp, 0, first=True)
        finish(1)
        for p in range(PIECES):
            to_mate(1, p).start()
            to_cross(1, p).wait_recv()
            forward(1, p).start()
        fold(tp, 1)
        fold(cross_tp, 0)
        fold(cross_tp, 1)
        for p in range(PIECES):
            to_mate(0, p).wait_recv()
        fold(mate_tp, 0)
        for p in range(PIECES):
            forward(0, p).wait_recv()
        fold(opposite_tp, 0)

        def place(p):
            return out.at[pl.ds(pl.multiple_of(mine * BLOCK + p * PIECE, PIECE), PIECE)]

        def keep(p):
            return pltpu.make_async_copy(obuf.at[mine, piece(p)], place(p), osem.at[p])

        def give(p):
            return pltpu.make_async_remote_copy(
                src_ref=obuf.at[1 - mine, piece(p)], dst_ref=place(p), send_sem=p2send.at[p],
                recv_sem=p2recv.at[p], device_id=cross,
            )

        for p in range(PIECES):
            to_mate(1, p).wait_recv()
            forward(1, p).wait_recv()
            at = slice(p * PIECE, (p + 1) * PIECE)
            for slot in range(2):
                last = oacc[slot, at]
                for source in (mate_tp, opposite_tp):
                    last += dot(hid[source, 1, at], wov[slot, source, DH : 2 * DH, :])
                obuf[slot, at] = last.astype(BF16)
            give(p).start()
            keep(p).start()

        wo_cross().wait_send()
        wo_mate().wait_send()
        wo_relay().wait_send()
        for r in range(n_tp):
            wo_hand(r).wait_send()
        for i, h in order:
            swap(i, h).wait_send()
        many(arcv, asend, arecv).wait_send()
        for h in range(2):
            many(rbuf.at[h], usend.at[h], urecv.at[h]).wait_send()
            many(sbuf.at[h], psend.at[h], precv.at[h]).wait_send()
            for p in range(PIECES):
                to_cross(h, p).wait_send()
                to_mate(h, p).wait_send()
                forward(h, p).wait_send()
        for p in range(PIECES):
            keep(p).wait()
            give(p).wait_send()
            give(p).wait_recv()

    return kernel


def solution(mesh):
    n_ctx, n_tp = mesh.shape["ctx"], mesh.shape["tp"]

    def on_device(tokens, query_weight, key_weight, value_weight, gate_weight, out_weight, log_decay):
        rows, depth = tokens.shape[1:]
        cols = query_weight.shape[1]
        out_rows = out_weight.shape[0]
        tables = rotation_rows(n_ctx, rows)
        vmem = lambda *shape, dtype=BF16: pltpu.VMEM(shape, dtype)
        dma = lambda *shape: pltpu.SemaphoreType.DMA(shape)
        anywhere = pl.BlockSpec(memory_space=pl.ANY)
        small = pl.BlockSpec(memory_space=pltpu.VMEM)
        result = pl.pallas_call(
            make_kernel(n_ctx, n_tp),
            out_shape=jax.ShapeDtypeStruct((rows, cols), BF16),
            in_specs=[anywhere] * 6 + [small] * 7,
            out_specs=anywhere,
            scratch_shapes=[
                vmem(rows, depth),
                vmem(4, 2, depth, DH),
                vmem(2, n_tp, out_rows, cols),
                vmem(2, rows, DH, dtype=F32),
                vmem(2, rows, DH),
                vmem(2, rows, DH),
                vmem(2, rows, DH),
                vmem(2, rows, DH),
                vmem(2, rows, DH, dtype=F32),
                vmem(2, 2, DH, DH, dtype=F32),
                vmem(2, n_ctx, 16, HALF),
                vmem(2, n_ctx, 16, HALF),
                vmem(2, n_ctx, 16, HALF),
                vmem(2, n_ctx, 16, HALF),
                vmem(8, HALF, dtype=F32),
                vmem(n_ctx, 8, HALF, dtype=F32),
                vmem(8, rows, dtype=F32),
                vmem(rows, 8, dtype=F32),
                vmem(rows, HALF, dtype=F32),
                vmem(rows, HALF, dtype=F32),
                vmem(2, DH, DH),
                vmem(n_tp, 2, BLOCK, DH),
                vmem(2, BLOCK, DH),
                vmem(2, BLOCK, cols, dtype=F32),
                vmem(2, BLOCK, cols),
                dma(2), dma(4, 2), dma(4, 2), dma(4, 2), dma(), dma(),
                dma(2), dma(2), dma(2), dma(2),
                dma(), dma(3), dma(3), dma(n_tp), dma(n_tp),
                dma(2, PIECES), dma(2, PIECES), dma(2, PIECES), dma(2, PIECES),
                dma(2, PIECES), dma(2, PIECES), dma(PIECES), dma(PIECES), dma(PIECES),
            ],
            compiler_params=pltpu.CompilerParams(
                collective_id=0, has_side_effects=True, vmem_limit_bytes=60 << 20
            ),
            name="retention",
        )(
            tokens[0], key_weight, value_weight, query_weight, gate_weight, out_weight,
            jnp.transpose(log_decay[0]), *tables,
        )
        return result[None]

    in_specs = (
        P("fsdp", "ctx", None),
        P("fsdp", "tp"),
        P("fsdp", "tp"),
        P("fsdp", "tp"),
        P("fsdp", "tp"),
        P("tp", "fsdp"),
        P("fsdp", "ctx", "tp"),
    )
    out_specs = P("fsdp", "ctx", "tp")
    return jax.shard_map(
        on_device, mesh=mesh, in_specs=in_specs, out_specs=out_specs, check_vma=False
    )
```

```python
import jax
import jax.numpy as jnp
import numpy as np
from jax import lax
from jax.experimental import pallas as pl
from jax.experimental.pallas import tpu as pltpu
from jax.sharding import PartitionSpec as P

DH = 256
HALF = DH // 2
BLOCK = 512
PIECES = 4
PIECE = BLOCK // PIECES
KEY, VALUE, QUERY, GATE = range(4)
F32, BF16 = jnp.float32, jnp.bfloat16


def dot(a, b):
    return jnp.dot(a, b, preferred_element_type=F32)


def rotation_rows(ctx_count, rows):
    frequency = 10000.0 ** (-np.arange(HALF) / HALF)
    tables = []
    for stride, count in ((32, rows // 32), (1, 32), (rows, ctx_count)):
        angles = (np.arange(count) * stride)[:, None] * frequency[None, :]
        tables += [np.cos(angles), np.sin(angles)]
    return np.concatenate(tables).astype(np.float32)


def make_kernel(n_ctx, n_tp):
    n_peers = n_ctx - 1

    def offset(i):
        return n_ctx // 2 + (i // 2 + lax.rem(i, 2)) * (1 - 2 * lax.rem(i, 2))

    def kernel(
        tok, wk, wv, wq, wg, wo, ld, turns, out,
        logs, table, tokv, wv_all, wov, acc, kb, vb, qb, gb, ret, ust, ubuf, rbuf, pbuf, sbuf,
        abuf, arcv, crow, ccol, cosv, sinv, stv, hid, away, oacc, obuf,
        isem, tsem, lsem, wsend, wrecv, asend, arecv, usend, urecv, psend, precv,
        wolocal, wosend, worecv, wofwd, wogot, crsend, crrecv, mtsend, mtrecv,
        fwsend, fwrecv, p2send, p2recv,
    ):
        ctx, tp, core = (lax.axis_index(n) for n in ("ctx", "tp", "fsdp"))
        rows = tok.shape[0]
        khalf = tok.shape[1] // 2
        partner = {"fsdp": 1 - core}
        mate_tp, cross_tp = tp + 1 - 2 * lax.rem(tp, 2), n_tp - 1 - tp
        opposite_tp = lax.rem(tp + 2, n_tp)
        mate, cross = {"tp": mate_tp}, {"tp": cross_tp}
        mine = tp // 2
        weights = (wk, wv, wq, wg)

        barrier = pltpu.get_barrier_semaphore()
        def greet(k, carry):
            pl.semaphore_signal(barrier, inc=1, device_id={"ctx": lax.rem(ctx + offset(k), n_ctx)})
            return carry

        lax.fori_loop(0, n_peers, greet, 0)
        pl.semaphore_signal(barrier, inc=1, device_id=partner)
        pl.semaphore_signal(barrier, inc=1, device_id=mate)
        pl.semaphore_signal(barrier, inc=1, device_id=cross)

        def log_copy():
            return pltpu.make_async_copy(ld, logs, isem.at[0])

        def table_copy():
            return pltpu.make_async_copy(turns, table, isem.at[1])

        log_copy().start()
        table_copy().start()

        own_rows = pl.ds(pl.multiple_of(core * khalf, khalf), khalf)
        other_rows = pl.ds(pl.multiple_of((1 - core) * khalf, khalf), khalf)

        def tok_copy(part):
            columns = own_rows if part == 0 else other_rows
            return pltpu.make_async_copy(tok.at[:, columns], tokv.at[:, columns], tsem.at[part])

        def own_copy(i, h):
            source = weights[i].at[:, h * DH : (h + 1) * DH]
            return pltpu.make_async_copy(source, wv_all.at[i, h, own_rows], lsem.at[i, h])

        order = [(KEY, 0), (VALUE, 0), (KEY, 1), (VALUE, 1), (QUERY, 0), (GATE, 0), (QUERY, 1), (GATE, 1)]
        tok_copy(0).start()
        for i, h in order[:2]:
            own_copy(i, h).start()
        tok_copy(1).start()
        for i, h in order[2:]:
            own_copy(i, h).start()

        crow[...] = jnp.zeros_like(crow)
        log_copy().wait()
        crow[0 : logs.shape[0], :] = logs[...]
        running = crow[...]
        lane = lax.rem(lax.broadcasted_iota(jnp.int32, running.shape, 1), BLOCK)
        step = 1
        while step < BLOCK:
            running = running + jnp.where(lane >= step, pltpu.roll(running, step, 1), 0.0)
            step *= 2
        crow[...] = running
        ccol[...] = running.T
        ends = [crow[:, (b + 1) * BLOCK - 1 : (b + 1) * BLOCK] for b in range(2)]
        total = ends[0] + ends[1]
        abuf[...] = jnp.broadcast_to(total, abuf.shape)
        arcv[ctx] = jnp.broadcast_to(total, abuf.shape)

        pl.semaphore_wait(barrier, 3 + n_peers)

        def swap(i, h):
            return pltpu.make_async_remote_copy(
                src_ref=weights[i].at[:, h * DH : (h + 1) * DH],
                dst_ref=wv_all.at[i, h, own_rows],
                send_sem=wsend.at[i, h],
                recv_sem=wrecv.at[i, h],
                device_id=partner,
            )

        for i, h in order:
            swap(i, h).start()

        def send_total(k, carry):
            pltpu.make_async_remote_copy(
                src_ref=abuf,
                dst_ref=arcv.at[ctx],
                send_sem=asend,
                recv_sem=arecv,
                device_id={"ctx": lax.rem(ctx + offset(k), n_ctx)},
            ).start()
            return carry

        lax.fori_loop(0, n_peers, send_total, 0)

        width = wo.shape[1] // 2
        group = lax.rem((tp + 1) // 2, 2)
        near = group + core * (1 - 2 * group)

        def wo_columns(index):
            return wo.at[:, pl.ds(pl.multiple_of(index * width, width), width)]

        def wo_own():
            return pltpu.make_async_copy(wo_columns(near), wov.at[core, tp], wolocal)

        def wo_copy(source, r, k, to):
            return pltpu.make_async_remote_copy(
                src_ref=source, dst_ref=wov.at[core, r], send_sem=wosend.at[k],
                recv_sem=worecv.at[k], device_id=to,
            )

        def wo_cross():
            return wo_copy(wo_columns(near), tp, 0, cross)

        def wo_mate():
            return wo_copy(wo_columns(1 - near), tp, 1, mate)

        def wo_relay():
            return wo_copy(wov.at[core, mate_tp], mate_tp, 2, cross)

        def wo_hand(r):
            return pltpu.make_async_remote_copy(
                src_ref=wov.at[core, r], dst_ref=wov.at[core, r], send_sem=wofwd.at[r],
                recv_sem=wogot.at[r], device_id=partner,
            )

        wo_own().start()
        wo_mate().start()
        wo_cross().start()

        table_copy().wait()
        fine = rows // 32
        cos_a, sin_a = table[0:fine, :], table[fine : 2 * fine, :]
        cos_b, sin_b = (table[2 * fine + k * 32 : 2 * fine + (k + 1) * 32, :] for k in range(2))
        base = 2 * fine + 64
        cc, sc = (table[pl.ds(base + k * n_ctx + ctx, 1), :] for k in range(2))
        base_cos, base_sin = cos_a * cc - sin_a * sc, sin_a * cc + cos_a * sc
        for a in range(rows // 32):
            ca, sa = base_cos[a : a + 1, :], base_sin[a : a + 1, :]
            cosv[a * 32 : (a + 1) * 32, :] = ca * cos_b - sa * sin_b
            sinv[a * 32 : (a + 1) * 32, :] = sa * cos_b + ca * sin_b

        def positions(b):
            return slice(b * BLOCK, (b + 1) * BLOCK)

        def own_product(i, h):
            own_copy(i, h).wait()
            acc[i] = dot(tokv[:, own_rows], wv_all[i, h, own_rows])

        def project(i, h, split=False):
            if split:
                swap(i, h).wait_recv()
                return acc[i] + dot(tokv[:, other_rows], wv_all[i, h, other_rows])
            own_copy(i, h).wait()
            swap(i, h).wait_recv()
            return dot(tokv[...], wv_all[i, h])

        def rotated(u):
            first, second = u[:, :HALF], u[:, HALF:]
            cosine, sine = cosv[...], sinv[...]
            return (first * cosine - second * sine).astype(BF16), (
                second * cosine + first * sine
            ).astype(BF16)

        def key_value(h):
            split = h == 0
            kb[h, :, :HALF], kb[h, :, HALF:] = rotated(project(KEY, h, split))
            vb[h] = project(VALUE, h, split).astype(BF16)

        def query(h):
            qb[h, :, :HALF], qb[h, :, HALF:] = rotated(project(QUERY, h))

        def gate(h):
            gb[h] = project(GATE, h).astype(BF16)

        def block_end(h, b):
            return crow[h : h + 1, (b + 1) * BLOCK - 1 : (b + 1) * BLOCK]

        def decay_column(h, b):
            return ccol[positions(b), h : h + 1]

        def states(h):
            for b in range(2):
                scale = jnp.exp(block_end(h, b) - decay_column(h, b))
                scaled = (kb[h, positions(b)].astype(F32) * scale).astype(BF16)
                ust[h, b] = lax.dot_general(
                    scaled, vb[h, positions(b)], (((0,), (0,)), ((), ())),
                    preferred_element_type=F32,
                )
            joined = (jnp.exp(block_end(h, 1)) * ust[h, 0] + ust[h, 1]).astype(BF16)
            for j in range(2):
                ubuf[h, j * 16 : (j + 1) * 16] = joined[:, j * HALF : (j + 1) * HALF].reshape(16, 16, HALF)
            rbuf[h, ctx] = ubuf[h, ctx]

            def send(k, carry):
                to = lax.rem(ctx + offset(k), n_ctx)
                pltpu.make_async_remote_copy(
                    src_ref=ubuf.at[h, to],
                    dst_ref=rbuf.at[h, ctx],
                    send_sem=usend.at[h],
                    recv_sem=urecv.at[h],
                    device_id={"ctx": to},
                ).start()
                return carry

            lax.fori_loop(0, n_peers, send, 0)

        def many(buffer, send_sem, recv_sem):
            part = buffer.at[pl.ds(0, n_peers)]
            return pltpu.make_async_remote_copy(
                src_ref=part, dst_ref=part, send_sem=send_sem, recv_sem=recv_sem,
                device_id={"ctx": lax.rem(ctx + 1, n_ctx)},
            )

        def scan(h):
            many(rbuf.at[h], usend.at[h], urecv.at[h]).wait_recv()

            before = jnp.zeros((16, HALF), F32)
            for d in range(n_ctx):
                pbuf[h, d] = before.astype(BF16)
                before = before * jnp.exp(arcv[d, h : h + 1, :]) + rbuf[h, d].astype(F32)
            sbuf[h, ctx] = pbuf[h, ctx]

            def send(k, carry):
                to = lax.rem(ctx + offset(k), n_ctx)
                pltpu.make_async_remote_copy(
                    src_ref=pbuf.at[h, to],
                    dst_ref=sbuf.at[h, ctx],
                    send_sem=psend.at[h],
                    recv_sem=precv.at[h],
                    device_id={"ctx": to},
                ).start()
                return carry

            lax.fori_loop(0, n_peers, send, 0)

        quarter = BLOCK // 2

        def intra(h):
            for b in range(2):
                for part in range(2):
                    start = b * BLOCK + part * quarter
                    extent = (part + 1) * quarter
                    mine = slice(start, start + quarter)
                    seen = slice(b * BLOCK, b * BLOCK + extent)
                    scores = lax.dot_general(
                        qb[h, mine], kb[h, seen], (((1,), (1,)), ((), ())),
                        preferred_element_type=F32,
                    )
                    t = lax.broadcasted_iota(jnp.int32, scores.shape, 0) + part * quarter
                    s = lax.broadcasted_iota(jnp.int32, scores.shape, 1)
                    differ = ccol[mine, h : h + 1] - crow[h : h + 1, seen]
                    decay = jnp.exp(jnp.where(t >= s, differ, 0.0))
                    mixed = jnp.where(t >= s, scores * decay, 0.0).astype(BF16)
                    ret[h, mine] = dot(mixed, vb[h, seen])

        def piece(p):
            return pl.ds(p * PIECE, PIECE)

        def hidden_copy(source, owner, h, p, sends, receives, to):
            return pltpu.make_async_remote_copy(
                src_ref=source, dst_ref=hid.at[owner, h, piece(p)], send_sem=sends.at[h, p],
                recv_sem=receives.at[h, p], device_id=to,
            )

        def to_cross(h, p):
            return hidden_copy(away.at[h, piece(p)], tp, h, p, crsend, crrecv, cross)

        def to_mate(h, p):
            return hidden_copy(hid.at[tp, h, piece(p)], tp, h, p, mtsend, mtrecv, mate)

        def forward(h, p):
            source = hid.at[cross_tp, h, piece(p)]
            return hidden_copy(source, cross_tp, h, p, fwsend, fwrecv, mate)

        def finish(h):
            many(sbuf.at[h], psend.at[h], precv.at[h]).wait_recv()
            state = jnp.concatenate(
                [sbuf[h, j * 16 : (j + 1) * 16].reshape(DH, HALF) for j in range(2)], axis=1
            )
            stv[0] = state
            stv[1] = (jnp.exp(block_end(h, 0)) * state.astype(F32) + ust[h, 0]).astype(BF16)

            def hidden(b):
                at = pl.ds(pl.multiple_of(b * BLOCK, BLOCK), BLOCK)
                inter = jnp.exp(ccol[at, h : h + 1]) * dot(qb[h, at], stv[b])
                retained = ret[h, at] + inter
                center = retained - jnp.mean(retained, axis=-1, keepdims=True)
                spread = jnp.mean(center * center, axis=-1, keepdims=True)
                normed = center * lax.rsqrt(spread + 1e-5)
                gates = gb[h, at].astype(F32)
                silu = gates / (1.0 + jnp.exp(-gates))
                return (silu * normed).astype(BF16)

            away[h] = hidden(1 - mine)
            for p in range(PIECES):
                to_cross(h, p).start()
            hid[tp, h] = hidden(mine)

        def fold(source, h, at=slice(None), first=False):
            for slot in range(2):
                product = dot(hid[source, h, at], wov[slot, source, h * DH : (h + 1) * DH, :])
                oacc[slot, at] = product if first else oacc[slot, at] + product

        tok_copy(0).wait()
        own_product(KEY, 0)
        own_product(VALUE, 0)
        tok_copy(1).wait()
        key_value(0)
        states(0)
        key_value(1)
        states(1)
        query(0)
        wo_mate().wait_recv()
        wo_relay().start()
        many(arcv, asend, arecv).wait_recv()
        scan(0)
        gate(0)
        intra(0)
        scan(1)
        query(1)
        gate(1)
        finish(0)
        for p in range(PIECES):
            to_mate(0, p).start()

        wo_own().wait()
        wo_cross().wait_recv()
        for r in (tp, mate_tp, cross_tp):
            wo_hand(r).start()
        intra(1)
        finish(1)
        for p in range(PIECES):
            to_cross(0, p).wait_recv()
            forward(0, p).start()
            if p == 0:
                wo_relay().wait_recv()
                wo_hand(opposite_tp).start()
                wo_hand(tp).wait_recv()
            if p == 1:
                fold(tp, 0, first=True)
                fold(tp, 1)
        for r in (cross_tp, mate_tp, opposite_tp):
            wo_hand(r).wait_recv()
        for p in range(PIECES):
            to_mate(1, p).start()
            to_cross(1, p).wait_recv()
            forward(1, p).start()
            if p == 0:
                fold(cross_tp, 0)
            if p == 1:
                for q in range(PIECES):
                    to_mate(0, q).wait_recv()
                fold(mate_tp, 0)
        fold(cross_tp, 1)
        for p in range(PIECES):
            forward(0, p).wait_recv()
        fold(opposite_tp, 0)

        def place(p):
            return pl.ds(pl.multiple_of(mine * BLOCK + p * PIECE, PIECE), PIECE)

        def give(p):
            return pltpu.make_async_remote_copy(
                src_ref=obuf.at[piece(p)], dst_ref=out.at[place(p)], send_sem=p2send.at[p],
                recv_sem=p2recv.at[p], device_id=cross,
            )

        for p in range(PIECES):
            to_mate(1, p).wait_recv()
            forward(1, p).wait_recv()
            at = slice(p * PIECE, (p + 1) * PIECE)

            def total_of(slot):
                last = oacc[slot, at]
                for source in (mate_tp, opposite_tp):
                    last += dot(hid[source, 1, at], wov[slot, source, DH : 2 * DH, :])
                return last.astype(BF16)

            obuf[at] = total_of(1 - mine)
            give(p).start()
            out[place(p)] = total_of(mine)

        wo_cross().wait_send()
        wo_mate().wait_send()
        wo_relay().wait_send()
        for r in range(n_tp):
            wo_hand(r).wait_send()
        for i, h in order:
            swap(i, h).wait_send()
        many(arcv, asend, arecv).wait_send()
        for h in range(2):
            many(rbuf.at[h], usend.at[h], urecv.at[h]).wait_send()
            many(sbuf.at[h], psend.at[h], precv.at[h]).wait_send()
            for p in range(PIECES):
                to_cross(h, p).wait_send()
                to_mate(h, p).wait_send()
                forward(h, p).wait_send()
        for p in range(PIECES):
            give(p).wait_send()
            give(p).wait_recv()

    return kernel


def solution(mesh):
    n_ctx, n_tp = mesh.shape["ctx"], mesh.shape["tp"]

    def on_device(tokens, query_weight, key_weight, value_weight, gate_weight, out_weight, log_decay):
        rows, depth = tokens.shape[1:]
        cols = query_weight.shape[1]
        out_rows = out_weight.shape[0]
        tables = rotation_rows(n_ctx, rows)
        vmem = lambda *shape, dtype=BF16: pltpu.VMEM(shape, dtype)
        dma = lambda *shape: pltpu.SemaphoreType.DMA(shape)
        anywhere = pl.BlockSpec(memory_space=pl.ANY)
        small = pl.BlockSpec(memory_space=pltpu.VMEM)
        result = pl.pallas_call(
            make_kernel(n_ctx, n_tp),
            out_shape=pltpu.VMEM((rows, cols), BF16),
            in_specs=[anywhere] * 8,
            out_specs=small,
            scratch_shapes=[
                vmem(cols // DH, rows, dtype=F32),
                vmem(*tables.shape, dtype=F32),
                vmem(rows, depth),
                vmem(4, 2, depth, DH),
                vmem(2, n_tp, out_rows, cols),
                vmem(2, rows, DH, dtype=F32),
                vmem(2, rows, DH),
                vmem(2, rows, DH),
                vmem(2, rows, DH),
                vmem(2, rows, DH),
                vmem(2, rows, DH, dtype=F32),
                vmem(2, 2, DH, DH, dtype=F32),
                vmem(2, n_ctx, 16, HALF),
                vmem(2, n_ctx, 16, HALF),
                vmem(2, n_ctx, 16, HALF),
                vmem(2, n_ctx, 16, HALF),
                vmem(8, HALF, dtype=F32),
                vmem(n_ctx, 8, HALF, dtype=F32),
                vmem(8, rows, dtype=F32),
                vmem(rows, 8, dtype=F32),
                vmem(rows, HALF, dtype=F32),
                vmem(rows, HALF, dtype=F32),
                vmem(2, DH, DH),
                vmem(n_tp, 2, BLOCK, DH),
                vmem(2, BLOCK, DH),
                vmem(2, BLOCK, cols, dtype=F32),
                vmem(BLOCK, cols),
                dma(2), dma(2), dma(4, 2), dma(4, 2), dma(4, 2), dma(), dma(),
                dma(2), dma(2), dma(2), dma(2),
                dma(), dma(3), dma(3), dma(n_tp), dma(n_tp),
                dma(2, PIECES), dma(2, PIECES), dma(2, PIECES), dma(2, PIECES),
                dma(2, PIECES), dma(2, PIECES), dma(PIECES), dma(PIECES),
            ],
            compiler_params=pltpu.CompilerParams(
                collective_id=0, has_side_effects=True, vmem_limit_bytes=60 << 20
            ),
            name="retention",
        )(
            tokens[0], key_weight, value_weight, query_weight, gate_weight, out_weight,
            jnp.transpose(log_decay[0]), tables,
        )
        return result[None]

    in_specs = (
        P("fsdp", "ctx", None),
        P("fsdp", "tp"),
        P("fsdp", "tp"),
        P("fsdp", "tp"),
        P("fsdp", "tp"),
        P("tp", "fsdp"),
        P("fsdp", "ctx", "tp"),
    )
    out_specs = P("fsdp", "ctx", "tp")
    return jax.shard_map(
        on_device, mesh=mesh, in_specs=in_specs, out_specs=out_specs, check_vma=False
    )
```

```python
import jax
import jax.numpy as jnp
import numpy as np
from jax import lax
from jax.experimental import pallas as pl
from jax.experimental.pallas import tpu as pltpu
from jax.sharding import PartitionSpec as P

DH = 256
HALF = DH // 2
BLOCK = 512
PIECES = 4
PIECE = BLOCK // PIECES
KEY, VALUE, QUERY, GATE = range(4)
F32, BF16 = jnp.float32, jnp.bfloat16


def dot(a, b):
    return jnp.dot(a, b, preferred_element_type=F32)


def rotation_rows(ctx_count, rows):
    frequency = 10000.0 ** (-np.arange(HALF) / HALF)
    tables = []
    for stride, count in ((32, rows // 32), (1, 32), (rows, ctx_count)):
        angles = (np.arange(count) * stride)[:, None] * frequency[None, :]
        tables += [np.cos(angles), np.sin(angles)]
    return np.concatenate(tables).astype(np.float32)


def make_kernel(n_ctx, n_tp):
    n_peers = n_ctx - 1

    def offset(i):
        return n_ctx // 2 + (i // 2 + lax.rem(i, 2)) * (1 - 2 * lax.rem(i, 2))

    def kernel(
        tok, wk, wv, wq, wg, wo, ld, turns, out,
        logs, table, tokv, wv_all, wov, acc, kb, vb, qb, gb, ret, ust, ubuf, rbuf, pbuf, sbuf,
        abuf, arcv, crow, ccol, cosv, sinv, stv, hid, away, oacc, obuf,
        isem, tsem, lsem, wsend, wrecv, asend, arecv, usend, urecv, psend, precv,
        wolocal, wosend, worecv, wofwd, wogot, crsend, crrecv, mtsend, mtrecv,
        fwsend, fwrecv, p2send, p2recv,
    ):
        ctx, tp, core = (lax.axis_index(n) for n in ("ctx", "tp", "fsdp"))
        rows = tok.shape[0]
        khalf = tok.shape[1] // 2
        partner = {"fsdp": 1 - core}
        mate_tp, cross_tp = tp + 1 - 2 * lax.rem(tp, 2), n_tp - 1 - tp
        opposite_tp = lax.rem(tp + 2, n_tp)
        mate, cross = {"tp": mate_tp}, {"tp": cross_tp}
        mine = tp // 2
        weights = (wk, wv, wq, wg)

        barrier = pltpu.get_barrier_semaphore()
        def greet(k, carry):
            pl.semaphore_signal(barrier, inc=1, device_id={"ctx": lax.rem(ctx + offset(k), n_ctx)})
            return carry

        lax.fori_loop(0, n_peers, greet, 0)
        pl.semaphore_signal(barrier, inc=1, device_id=partner)
        pl.semaphore_signal(barrier, inc=1, device_id=mate)
        pl.semaphore_signal(barrier, inc=1, device_id=cross)

        def log_copy():
            return pltpu.make_async_copy(ld, logs, isem.at[0])

        def table_copy():
            return pltpu.make_async_copy(turns, table, isem.at[1])

        log_copy().start()
        table_copy().start()

        own_rows = pl.ds(pl.multiple_of(core * khalf, khalf), khalf)
        other_rows = pl.ds(pl.multiple_of((1 - core) * khalf, khalf), khalf)

        def tok_copy(part):
            columns = own_rows if part == 0 else other_rows
            return pltpu.make_async_copy(tok.at[:, columns], tokv.at[:, columns], tsem.at[part])

        def own_copy(i, h):
            source = weights[i].at[:, h * DH : (h + 1) * DH]
            return pltpu.make_async_copy(source, wv_all.at[i, h, own_rows], lsem.at[i, h])

        order = [(KEY, 0), (VALUE, 0), (KEY, 1), (VALUE, 1), (QUERY, 0), (GATE, 0), (QUERY, 1), (GATE, 1)]
        tok_copy(0).start()
        for i, h in order[:2]:
            own_copy(i, h).start()
        tok_copy(1).start()
        for i, h in order[2:]:
            own_copy(i, h).start()

        crow[...] = jnp.zeros_like(crow)
        log_copy().wait()
        crow[0 : logs.shape[0], :] = logs[...]
        running = crow[...]
        lane = lax.rem(lax.broadcasted_iota(jnp.int32, running.shape, 1), BLOCK)
        step = 1
        while step < BLOCK:
            running = running + jnp.where(lane >= step, pltpu.roll(running, step, 1), 0.0)
            step *= 2
        crow[...] = running
        ccol[...] = running.T
        ends = [crow[:, (b + 1) * BLOCK - 1 : (b + 1) * BLOCK] for b in range(2)]
        total = ends[0] + ends[1]
        abuf[...] = jnp.broadcast_to(total, abuf.shape)
        arcv[ctx] = jnp.broadcast_to(total, abuf.shape)

        pl.semaphore_wait(barrier, 3 + n_peers)

        def swap(i, h):
            return pltpu.make_async_remote_copy(
                src_ref=weights[i].at[:, h * DH : (h + 1) * DH],
                dst_ref=wv_all.at[i, h, own_rows],
                send_sem=wsend.at[i, h],
                recv_sem=wrecv.at[i, h],
                device_id=partner,
            )

        for i, h in order:
            swap(i, h).start()

        def send_total(k, carry):
            pltpu.make_async_remote_copy(
                src_ref=abuf,
                dst_ref=arcv.at[ctx],
                send_sem=asend,
                recv_sem=arecv,
                device_id={"ctx": lax.rem(ctx + offset(k), n_ctx)},
            ).start()
            return carry

        lax.fori_loop(0, n_peers, send_total, 0)

        width = wo.shape[1] // 2
        group = lax.rem((tp + 1) // 2, 2)
        near = group + core * (1 - 2 * group)

        def wo_columns(index):
            return wo.at[:, pl.ds(pl.multiple_of(index * width, width), width)]

        def wo_own():
            return pltpu.make_async_copy(wo_columns(near), wov.at[core, tp], wolocal)

        def wo_copy(source, target, k, to):
            return pltpu.make_async_remote_copy(
                src_ref=source, dst_ref=target, send_sem=wosend.at[k],
                recv_sem=worecv.at[k], device_id=to,
            )

        def wo_cross():
            return wo_copy(wo_columns(near), wov.at[core, tp], 4, cross)

        part_rows = wo.shape[0] // 2

        def wo_mate(part):
            at = pl.ds(part * part_rows, part_rows)
            columns = pl.ds(pl.multiple_of((1 - near) * width, width), width)
            return wo_copy(wo.at[at, columns], wov.at[core, tp, at], part, mate)

        def wo_relay(part):
            block = wov.at[core, mate_tp, pl.ds(part * part_rows, part_rows)]
            return wo_copy(block, block, 2 + part, cross)

        def wo_hand(r):
            return pltpu.make_async_remote_copy(
                src_ref=wov.at[core, r], dst_ref=wov.at[core, r], send_sem=wofwd.at[r],
                recv_sem=wogot.at[r], device_id=partner,
            )

        wo_own().start()
        for part in range(2):
            wo_mate(part).start()
        wo_cross().start()

        table_copy().wait()
        fine = rows // 32
        cos_a, sin_a = table[0:fine, :], table[fine : 2 * fine, :]
        cos_b, sin_b = (table[2 * fine + k * 32 : 2 * fine + (k + 1) * 32, :] for k in range(2))
        base = 2 * fine + 64
        cc, sc = (table[pl.ds(base + k * n_ctx + ctx, 1), :] for k in range(2))
        base_cos, base_sin = cos_a * cc - sin_a * sc, sin_a * cc + cos_a * sc
        for a in range(rows // 32):
            ca, sa = base_cos[a : a + 1, :], base_sin[a : a + 1, :]
            cosv[a * 32 : (a + 1) * 32, :] = ca * cos_b - sa * sin_b
            sinv[a * 32 : (a + 1) * 32, :] = sa * cos_b + ca * sin_b

        def positions(b):
            return slice(b * BLOCK, (b + 1) * BLOCK)

        def own_product(i, h):
            own_copy(i, h).wait()
            acc[i] = dot(tokv[:, own_rows], wv_all[i, h, own_rows])

        def project(i, h, split=False):
            if split:
                swap(i, h).wait_recv()
                return acc[i] + dot(tokv[:, other_rows], wv_all[i, h, other_rows])
            own_copy(i, h).wait()
            swap(i, h).wait_recv()
            return dot(tokv[...], wv_all[i, h])

        def rotated(u):
            first, second = u[:, :HALF], u[:, HALF:]
            cosine, sine = cosv[...], sinv[...]
            return (first * cosine - second * sine).astype(BF16), (
                second * cosine + first * sine
            ).astype(BF16)

        def key_value(h):
            split = h == 0
            kb[h, :, :HALF], kb[h, :, HALF:] = rotated(project(KEY, h, split))
            vb[h] = project(VALUE, h, split).astype(BF16)

        def query(h):
            qb[h, :, :HALF], qb[h, :, HALF:] = rotated(project(QUERY, h))

        def gate(h):
            gb[h] = project(GATE, h).astype(BF16)

        def block_end(h, b):
            return crow[h : h + 1, (b + 1) * BLOCK - 1 : (b + 1) * BLOCK]

        def decay_column(h, b):
            return ccol[positions(b), h : h + 1]

        def states(h):
            for b in range(2):
                scale = jnp.exp(block_end(h, b) - decay_column(h, b))
                scaled = (kb[h, positions(b)].astype(F32) * scale).astype(BF16)
                ust[h, b] = lax.dot_general(
                    scaled, vb[h, positions(b)], (((0,), (0,)), ((), ())),
                    preferred_element_type=F32,
                )
            joined = (jnp.exp(block_end(h, 1)) * ust[h, 0] + ust[h, 1]).astype(BF16)
            for j in range(2):
                ubuf[h, j * 16 : (j + 1) * 16] = joined[:, j * HALF : (j + 1) * HALF].reshape(16, 16, HALF)
            rbuf[h, ctx] = ubuf[h, ctx]

            def send(k, carry):
                to = lax.rem(ctx + offset(k), n_ctx)
                pltpu.make_async_remote_copy(
                    src_ref=ubuf.at[h, to],
                    dst_ref=rbuf.at[h, ctx],
                    send_sem=usend.at[h],
                    recv_sem=urecv.at[h],
                    device_id={"ctx": to},
                ).start()
                return carry

            lax.fori_loop(0, n_peers, send, 0)

        def many(buffer, send_sem, recv_sem):
            part = buffer.at[pl.ds(0, n_peers)]
            return pltpu.make_async_remote_copy(
                src_ref=part, dst_ref=part, send_sem=send_sem, recv_sem=recv_sem,
                device_id={"ctx": lax.rem(ctx + 1, n_ctx)},
            )

        def scan(h):
            many(rbuf.at[h], usend.at[h], urecv.at[h]).wait_recv()

            before = jnp.zeros((16, HALF), F32)
            for d in range(n_ctx):
                pbuf[h, d] = before.astype(BF16)
                before = before * jnp.exp(arcv[d, h : h + 1, :]) + rbuf[h, d].astype(F32)
            sbuf[h, ctx] = pbuf[h, ctx]

            def send(k, carry):
                to = lax.rem(ctx + offset(k), n_ctx)
                pltpu.make_async_remote_copy(
                    src_ref=pbuf.at[h, to],
                    dst_ref=sbuf.at[h, ctx],
                    send_sem=psend.at[h],
                    recv_sem=precv.at[h],
                    device_id={"ctx": to},
                ).start()
                return carry

            lax.fori_loop(0, n_peers, send, 0)

        quarter = BLOCK // 2

        def intra(h):
            for b in range(2):
                for part in range(2):
                    start = b * BLOCK + part * quarter
                    extent = (part + 1) * quarter
                    mine = slice(start, start + quarter)
                    seen = slice(b * BLOCK, b * BLOCK + extent)
                    scores = lax.dot_general(
                        qb[h, mine], kb[h, seen], (((1,), (1,)), ((), ())),
                        preferred_element_type=F32,
                    )
                    t = lax.broadcasted_iota(jnp.int32, scores.shape, 0) + part * quarter
                    s = lax.broadcasted_iota(jnp.int32, scores.shape, 1)
                    differ = ccol[mine, h : h + 1] - crow[h : h + 1, seen]
                    decay = jnp.exp(jnp.where(t >= s, differ, 0.0))
                    mixed = jnp.where(t >= s, scores * decay, 0.0).astype(BF16)
                    ret[h, mine] = dot(mixed, vb[h, seen])

        def piece(p):
            return pl.ds(p * PIECE, PIECE)

        def hidden_copy(source, owner, h, p, sends, receives, to):
            return pltpu.make_async_remote_copy(
                src_ref=source, dst_ref=hid.at[owner, h, piece(p)], send_sem=sends.at[h, p],
                recv_sem=receives.at[h, p], device_id=to,
            )

        def to_cross(h, p):
            return hidden_copy(away.at[h, piece(p)], tp, h, p, crsend, crrecv, cross)

        def to_mate(h, p):
            return hidden_copy(hid.at[tp, h, piece(p)], tp, h, p, mtsend, mtrecv, mate)

        def forward(h, p):
            source = hid.at[cross_tp, h, piece(p)]
            return hidden_copy(source, cross_tp, h, p, fwsend, fwrecv, mate)

        def finish(h):
            many(sbuf.at[h], psend.at[h], precv.at[h]).wait_recv()
            state = jnp.concatenate(
                [sbuf[h, j * 16 : (j + 1) * 16].reshape(DH, HALF) for j in range(2)], axis=1
            )
            stv[0] = state
            stv[1] = (jnp.exp(block_end(h, 0)) * state.astype(F32) + ust[h, 0]).astype(BF16)

            def hidden(b):
                at = pl.ds(pl.multiple_of(b * BLOCK, BLOCK), BLOCK)
                inter = jnp.exp(ccol[at, h : h + 1]) * dot(qb[h, at], stv[b])
                retained = ret[h, at] + inter
                center = retained - jnp.mean(retained, axis=-1, keepdims=True)
                spread = jnp.mean(center * center, axis=-1, keepdims=True)
                normed = center * lax.rsqrt(spread + 1e-5)
                gates = gb[h, at].astype(F32)
                silu = gates / (1.0 + jnp.exp(-gates))
                return (silu * normed).astype(BF16)

            away[h] = hidden(1 - mine)
            for p in range(PIECES):
                to_cross(h, p).start()
            hid[tp, h] = hidden(mine)

        def fold(source, h, at=slice(None), first=False):
            for slot in range(2):
                product = dot(hid[source, h, at], wov[slot, source, h * DH : (h + 1) * DH, :])
                oacc[slot, at] = product if first else oacc[slot, at] + product

        tok_copy(0).wait()
        own_product(KEY, 0)
        own_product(VALUE, 0)
        tok_copy(1).wait()
        key_value(0)
        states(0)
        key_value(1)
        states(1)
        query(0)
        wo_mate(0).wait_recv()
        wo_relay(0).start()
        many(arcv, asend, arecv).wait_recv()
        scan(0)
        gate(0)
        wo_mate(1).wait_recv()
        wo_relay(1).start()
        intra(0)
        scan(1)
        query(1)
        finish(0)
        for p in range(PIECES):
            to_mate(0, p).start()

        wo_own().wait()
        wo_cross().wait_recv()
        for r in (tp, mate_tp, cross_tp):
            wo_hand(r).start()
        gate(1)
        intra(1)
        finish(1)
        for p in range(PIECES):
            to_cross(0, p).wait_recv()
            forward(0, p).start()
            if p == 0:
                for part in range(2):
                    wo_relay(part).wait_recv()
                wo_hand(opposite_tp).start()
                wo_hand(tp).wait_recv()
            if p == 1:
                fold(tp, 0, first=True)
                fold(tp, 1)
        for r in (cross_tp, mate_tp, opposite_tp):
            wo_hand(r).wait_recv()
        for p in range(PIECES):
            to_mate(1, p).start()
            to_cross(1, p).wait_recv()
            forward(1, p).start()
            if p == 0:
                fold(cross_tp, 0)
            if p == 1:
                for q in range(PIECES):
                    to_mate(0, q).wait_recv()
                fold(mate_tp, 0)
        fold(cross_tp, 1)
        for p in range(PIECES):
            forward(0, p).wait_recv()
        fold(opposite_tp, 0)

        def place(p):
            return pl.ds(pl.multiple_of(mine * BLOCK + p * PIECE, PIECE), PIECE)

        def give(p):
            return pltpu.make_async_remote_copy(
                src_ref=obuf.at[piece(p)], dst_ref=out.at[place(p)], send_sem=p2send.at[p],
                recv_sem=p2recv.at[p], device_id=cross,
            )

        for p in range(PIECES):
            to_mate(1, p).wait_recv()
            forward(1, p).wait_recv()
            at = slice(p * PIECE, (p + 1) * PIECE)

            def total_of(slot):
                last = oacc[slot, at]
                for source in (mate_tp, opposite_tp):
                    last += dot(hid[source, 1, at], wov[slot, source, DH : 2 * DH, :])
                return last.astype(BF16)

            obuf[at] = total_of(1 - mine)
            give(p).start()
            out[place(p)] = total_of(mine)

        wo_cross().wait_send()
        for part in range(2):
            wo_mate(part).wait_send()
            wo_relay(part).wait_send()
        for r in range(n_tp):
            wo_hand(r).wait_send()
        for i, h in order:
            swap(i, h).wait_send()
        many(arcv, asend, arecv).wait_send()
        for h in range(2):
            many(rbuf.at[h], usend.at[h], urecv.at[h]).wait_send()
            many(sbuf.at[h], psend.at[h], precv.at[h]).wait_send()
            for p in range(PIECES):
                to_cross(h, p).wait_send()
                to_mate(h, p).wait_send()
                forward(h, p).wait_send()
        for p in range(PIECES):
            give(p).wait_send()
            give(p).wait_recv()

    return kernel


def solution(mesh):
    n_ctx, n_tp = mesh.shape["ctx"], mesh.shape["tp"]

    def on_device(tokens, query_weight, key_weight, value_weight, gate_weight, out_weight, log_decay):
        rows, depth = tokens.shape[1:]
        cols = query_weight.shape[1]
        out_rows = out_weight.shape[0]
        tables = rotation_rows(n_ctx, rows)
        vmem = lambda *shape, dtype=BF16: pltpu.VMEM(shape, dtype)
        dma = lambda *shape: pltpu.SemaphoreType.DMA(shape)
        anywhere = pl.BlockSpec(memory_space=pl.ANY)
        small = pl.BlockSpec(memory_space=pltpu.VMEM)
        result = pl.pallas_call(
            make_kernel(n_ctx, n_tp),
            out_shape=pltpu.VMEM((rows, cols), BF16),
            in_specs=[anywhere] * 8,
            out_specs=small,
            scratch_shapes=[
                vmem(cols // DH, rows, dtype=F32),
                vmem(*tables.shape, dtype=F32),
                vmem(rows, depth),
                vmem(4, 2, depth, DH),
                vmem(2, n_tp, out_rows, cols),
                vmem(2, rows, DH, dtype=F32),
                vmem(2, rows, DH),
                vmem(2, rows, DH),
                vmem(2, rows, DH),
                vmem(2, rows, DH),
                vmem(2, rows, DH, dtype=F32),
                vmem(2, 2, DH, DH, dtype=F32),
                vmem(2, n_ctx, 16, HALF),
                vmem(2, n_ctx, 16, HALF),
                vmem(2, n_ctx, 16, HALF),
                vmem(2, n_ctx, 16, HALF),
                vmem(8, HALF, dtype=F32),
                vmem(n_ctx, 8, HALF, dtype=F32),
                vmem(8, rows, dtype=F32),
                vmem(rows, 8, dtype=F32),
                vmem(rows, HALF, dtype=F32),
                vmem(rows, HALF, dtype=F32),
                vmem(2, DH, DH),
                vmem(n_tp, 2, BLOCK, DH),
                vmem(2, BLOCK, DH),
                vmem(2, BLOCK, cols, dtype=F32),
                vmem(BLOCK, cols),
                dma(2), dma(2), dma(4, 2), dma(4, 2), dma(4, 2), dma(), dma(),
                dma(2), dma(2), dma(2), dma(2),
                dma(), dma(5), dma(5), dma(n_tp), dma(n_tp),
                dma(2, PIECES), dma(2, PIECES), dma(2, PIECES), dma(2, PIECES),
                dma(2, PIECES), dma(2, PIECES), dma(PIECES), dma(PIECES),
            ],
            compiler_params=pltpu.CompilerParams(
                collective_id=0, has_side_effects=True, vmem_limit_bytes=60 << 20
            ),
            name="retention",
        )(
            tokens[0], key_weight, value_weight, query_weight, gate_weight, out_weight,
            jnp.transpose(log_decay[0]), tables,
        )
        return result[None]

    in_specs = (
        P("fsdp", "ctx", None),
        P("fsdp", "tp"),
        P("fsdp", "tp"),
        P("fsdp", "tp"),
        P("fsdp", "tp"),
        P("tp", "fsdp"),
        P("fsdp", "ctx", "tp"),
    )
    out_specs = P("fsdp", "ctx", "tp")
    return jax.shard_map(
        on_device, mesh=mesh, in_specs=in_specs, out_specs=out_specs, check_vma=False
    )
```

```python
import jax
import jax.numpy as jnp
import numpy as np
from jax import lax
from jax.experimental import pallas as pl
from jax.experimental.pallas import tpu as pltpu
from jax.sharding import PartitionSpec as P

DH = 256
HALF = DH // 2
BLOCK = 512
PIECES = 8
PIECE = BLOCK // PIECES
KEY, VALUE, QUERY, GATE = range(4)
F32, BF16 = jnp.float32, jnp.bfloat16


def dot(a, b):
    return jnp.dot(a, b, preferred_element_type=F32)


def rotation_rows(ctx_count, rows):
    frequency = 10000.0 ** (-np.arange(HALF) / HALF)
    tables = []
    for stride, count in ((32, rows // 32), (1, 32), (rows, ctx_count)):
        angles = (np.arange(count) * stride)[:, None] * frequency[None, :]
        tables += [np.cos(angles), np.sin(angles)]
    return np.concatenate(tables).astype(np.float32)


def make_kernel(n_ctx, n_tp):
    n_peers = n_ctx - 1

    def offset(i):
        return n_ctx // 2 + (i // 2 + lax.rem(i, 2)) * (1 - 2 * lax.rem(i, 2))

    def kernel(
        tok, wk, wv, wq, wg, wo, ld, turns, out,
        logs, table, tokv, wv_all, wov, acc, kb, vb, qb, gb, ret, ust, ubuf, rbuf, pbuf, sbuf,
        abuf, arcv, crow, ccol, cosv, sinv, stv, hid, away, oacc, obuf,
        isem, tsem, lsem, wsend, wrecv, asend, arecv, usend, urecv, psend, precv,
        wolocal, wosend, worecv, wofwd, wogot, crsend, crrecv, mtsend, mtrecv,
        fwsend, fwrecv, p2send, p2recv,
    ):
        ctx, tp, core = (lax.axis_index(n) for n in ("ctx", "tp", "fsdp"))
        rows = tok.shape[0]
        khalf = tok.shape[1] // 2
        partner = {"fsdp": 1 - core}
        mate_tp, cross_tp = tp + 1 - 2 * lax.rem(tp, 2), n_tp - 1 - tp
        opposite_tp = lax.rem(tp + 2, n_tp)
        mate, cross = {"tp": mate_tp}, {"tp": cross_tp}
        mine = tp // 2
        weights = (wk, wv, wq, wg)

        barrier = pltpu.get_barrier_semaphore()
        def greet(k, carry):
            pl.semaphore_signal(barrier, inc=1, device_id={"ctx": lax.rem(ctx + offset(k), n_ctx)})
            return carry

        lax.fori_loop(0, n_peers, greet, 0)
        pl.semaphore_signal(barrier, inc=1, device_id=partner)
        pl.semaphore_signal(barrier, inc=1, device_id=mate)
        pl.semaphore_signal(barrier, inc=1, device_id=cross)

        def log_copy():
            return pltpu.make_async_copy(ld, logs, isem.at[0])

        def table_copy():
            return pltpu.make_async_copy(turns, table, isem.at[1])

        log_copy().start()
        table_copy().start()

        own_rows = pl.ds(pl.multiple_of(core * khalf, khalf), khalf)
        other_rows = pl.ds(pl.multiple_of((1 - core) * khalf, khalf), khalf)

        def tok_copy(part):
            columns = own_rows if part == 0 else other_rows
            return pltpu.make_async_copy(tok.at[:, columns], tokv.at[:, columns], tsem.at[part])

        def own_copy(i, h):
            source = weights[i].at[:, h * DH : (h + 1) * DH]
            return pltpu.make_async_copy(source, wv_all.at[i, h, own_rows], lsem.at[i, h])

        order = [(KEY, 0), (VALUE, 0), (KEY, 1), (VALUE, 1), (QUERY, 0), (GATE, 0), (QUERY, 1), (GATE, 1)]
        tok_copy(0).start()
        for i, h in order[:2]:
            own_copy(i, h).start()
        tok_copy(1).start()
        for i, h in order[2:]:
            own_copy(i, h).start()

        crow[...] = jnp.zeros_like(crow)
        log_copy().wait()
        crow[0 : logs.shape[0], :] = logs[...]
        running = crow[...]
        lane = lax.rem(lax.broadcasted_iota(jnp.int32, running.shape, 1), BLOCK)
        step = 1
        while step < BLOCK:
            running = running + jnp.where(lane >= step, pltpu.roll(running, step, 1), 0.0)
            step *= 2
        crow[...] = running
        ccol[...] = running.T
        ends = [crow[:, (b + 1) * BLOCK - 1 : (b + 1) * BLOCK] for b in range(2)]
        total = ends[0] + ends[1]
        abuf[...] = jnp.broadcast_to(total, abuf.shape)
        arcv[ctx] = jnp.broadcast_to(total, abuf.shape)

        pl.semaphore_wait(barrier, 3 + n_peers)

        def swap(i, h):
            return pltpu.make_async_remote_copy(
                src_ref=weights[i].at[:, h * DH : (h + 1) * DH],
                dst_ref=wv_all.at[i, h, own_rows],
                send_sem=wsend.at[i, h],
                recv_sem=wrecv.at[i, h],
                device_id=partner,
            )

        for i, h in order:
            swap(i, h).start()

        def send_total(k, carry):
            pltpu.make_async_remote_copy(
                src_ref=abuf,
                dst_ref=arcv.at[ctx],
                send_sem=asend,
                recv_sem=arecv,
                device_id={"ctx": lax.rem(ctx + offset(k), n_ctx)},
            ).start()
            return carry

        lax.fori_loop(0, n_peers, send_total, 0)

        width = wo.shape[1] // 2
        group = lax.rem((tp + 1) // 2, 2)
        near = group + core * (1 - 2 * group)

        def wo_columns(index):
            return wo.at[:, pl.ds(pl.multiple_of(index * width, width), width)]

        def wo_own():
            return pltpu.make_async_copy(wo_columns(near), wov.at[core, tp], wolocal)

        def wo_copy(source, target, k, to):
            return pltpu.make_async_remote_copy(
                src_ref=source, dst_ref=target, send_sem=wosend.at[k],
                recv_sem=worecv.at[k], device_id=to,
            )

        def wo_cross():
            return wo_copy(wo_columns(near), wov.at[core, tp], 4, cross)

        part_rows = wo.shape[0] // 2

        def wo_mate(part):
            at = pl.ds(part * part_rows, part_rows)
            columns = pl.ds(pl.multiple_of((1 - near) * width, width), width)
            return wo_copy(wo.at[at, columns], wov.at[core, tp, at], part, mate)

        def wo_relay(part):
            block = wov.at[core, mate_tp, pl.ds(part * part_rows, part_rows)]
            return wo_copy(block, block, 2 + part, cross)

        def wo_hand(r):
            return pltpu.make_async_remote_copy(
                src_ref=wov.at[core, r], dst_ref=wov.at[core, r], send_sem=wofwd.at[r],
                recv_sem=wogot.at[r], device_id=partner,
            )

        wo_own().start()
        for part in range(2):
            wo_mate(part).start()
        wo_cross().start()

        table_copy().wait()
        fine = rows // 32
        cos_a, sin_a = table[0:fine, :], table[fine : 2 * fine, :]
        cos_b, sin_b = (table[2 * fine + k * 32 : 2 * fine + (k + 1) * 32, :] for k in range(2))
        base = 2 * fine + 64
        cc, sc = (table[pl.ds(base + k * n_ctx + ctx, 1), :] for k in range(2))
        base_cos, base_sin = cos_a * cc - sin_a * sc, sin_a * cc + cos_a * sc
        for a in range(rows // 32):
            ca, sa = base_cos[a : a + 1, :], base_sin[a : a + 1, :]
            cosv[a * 32 : (a + 1) * 32, :] = ca * cos_b - sa * sin_b
            sinv[a * 32 : (a + 1) * 32, :] = sa * cos_b + ca * sin_b

        def positions(b):
            return slice(b * BLOCK, (b + 1) * BLOCK)

        def own_product(i, h):
            own_copy(i, h).wait()
            acc[i] = dot(tokv[:, own_rows], wv_all[i, h, own_rows])

        def project(i, h, split=False):
            if split:
                swap(i, h).wait_recv()
                return acc[i] + dot(tokv[:, other_rows], wv_all[i, h, other_rows])
            own_copy(i, h).wait()
            swap(i, h).wait_recv()
            return dot(tokv[...], wv_all[i, h])

        def rotated(u):
            first, second = u[:, :HALF], u[:, HALF:]
            cosine, sine = cosv[...], sinv[...]
            return (first * cosine - second * sine).astype(BF16), (
                second * cosine + first * sine
            ).astype(BF16)

        def key_value(h):
            split = h == 0
            kb[h, :, :HALF], kb[h, :, HALF:] = rotated(project(KEY, h, split))
            vb[h] = project(VALUE, h, split).astype(BF16)

        def query(h):
            qb[h, :, :HALF], qb[h, :, HALF:] = rotated(project(QUERY, h))

        def gate(h):
            gb[h] = project(GATE, h).astype(BF16)

        def block_end(h, b):
            return crow[h : h + 1, (b + 1) * BLOCK - 1 : (b + 1) * BLOCK]

        def decay_column(h, b):
            return ccol[positions(b), h : h + 1]

        def states(h):
            for b in range(2):
                scale = jnp.exp(block_end(h, b) - decay_column(h, b))
                scaled = (kb[h, positions(b)].astype(F32) * scale).astype(BF16)
                ust[h, b] = lax.dot_general(
                    scaled, vb[h, positions(b)], (((0,), (0,)), ((), ())),
                    preferred_element_type=F32,
                )
            joined = (jnp.exp(block_end(h, 1)) * ust[h, 0] + ust[h, 1]).astype(BF16)
            for j in range(2):
                ubuf[h, j * 16 : (j + 1) * 16] = joined[:, j * HALF : (j + 1) * HALF].reshape(16, 16, HALF)
            rbuf[h, ctx] = ubuf[h, ctx]

            def send(k, carry):
                to = lax.rem(ctx + offset(k), n_ctx)
                pltpu.make_async_remote_copy(
                    src_ref=ubuf.at[h, to],
                    dst_ref=rbuf.at[h, ctx],
                    send_sem=usend.at[h],
                    recv_sem=urecv.at[h],
                    device_id={"ctx": to},
                ).start()
                return carry

            lax.fori_loop(0, n_peers, send, 0)

        def many(buffer, send_sem, recv_sem):
            part = buffer.at[pl.ds(0, n_peers)]
            return pltpu.make_async_remote_copy(
                src_ref=part, dst_ref=part, send_sem=send_sem, recv_sem=recv_sem,
                device_id={"ctx": lax.rem(ctx + 1, n_ctx)},
            )

        def scan(h):
            many(rbuf.at[h], usend.at[h], urecv.at[h]).wait_recv()

            before = jnp.zeros((16, HALF), F32)
            for d in range(n_ctx):
                pbuf[h, d] = before.astype(BF16)
                before = before * jnp.exp(arcv[d, h : h + 1, :]) + rbuf[h, d].astype(F32)
            sbuf[h, ctx] = pbuf[h, ctx]

            def send(k, carry):
                to = lax.rem(ctx + offset(k), n_ctx)
                pltpu.make_async_remote_copy(
                    src_ref=pbuf.at[h, to],
                    dst_ref=sbuf.at[h, ctx],
                    send_sem=psend.at[h],
                    recv_sem=precv.at[h],
                    device_id={"ctx": to},
                ).start()
                return carry

            lax.fori_loop(0, n_peers, send, 0)

        quarter = BLOCK // 2

        def intra(h):
            for b in range(2):
                for part in range(2):
                    start = b * BLOCK + part * quarter
                    extent = (part + 1) * quarter
                    mine = slice(start, start + quarter)
                    seen = slice(b * BLOCK, b * BLOCK + extent)
                    scores = lax.dot_general(
                        qb[h, mine], kb[h, seen], (((1,), (1,)), ((), ())),
                        preferred_element_type=F32,
                    )
                    t = lax.broadcasted_iota(jnp.int32, scores.shape, 0) + part * quarter
                    s = lax.broadcasted_iota(jnp.int32, scores.shape, 1)
                    differ = ccol[mine, h : h + 1] - crow[h : h + 1, seen]
                    decay = jnp.exp(jnp.where(t >= s, differ, 0.0))
                    mixed = jnp.where(t >= s, scores * decay, 0.0).astype(BF16)
                    ret[h, mine] = dot(mixed, vb[h, seen])

        def piece(p):
            return pl.ds(p * PIECE, PIECE)

        def hidden_copy(source, owner, h, p, sends, receives, to):
            return pltpu.make_async_remote_copy(
                src_ref=source, dst_ref=hid.at[owner, h, piece(p)], send_sem=sends.at[h, p],
                recv_sem=receives.at[h, p], device_id=to,
            )

        def to_cross(h, p):
            return hidden_copy(away.at[h, piece(p)], tp, h, p, crsend, crrecv, cross)

        def to_mate(h, p):
            return hidden_copy(hid.at[tp, h, piece(p)], tp, h, p, mtsend, mtrecv, mate)

        def forward(h, p):
            source = hid.at[cross_tp, h, piece(p)]
            return hidden_copy(source, cross_tp, h, p, fwsend, fwrecv, mate)

        def finish(h):
            many(sbuf.at[h], psend.at[h], precv.at[h]).wait_recv()
            state = jnp.concatenate(
                [sbuf[h, j * 16 : (j + 1) * 16].reshape(DH, HALF) for j in range(2)], axis=1
            )
            stv[0] = state
            stv[1] = (jnp.exp(block_end(h, 0)) * state.astype(F32) + ust[h, 0]).astype(BF16)

            def hidden(b):
                at = pl.ds(pl.multiple_of(b * BLOCK, BLOCK), BLOCK)
                inter = jnp.exp(ccol[at, h : h + 1]) * dot(qb[h, at], stv[b])
                retained = ret[h, at] + inter
                center = retained - jnp.mean(retained, axis=-1, keepdims=True)
                spread = jnp.mean(center * center, axis=-1, keepdims=True)
                normed = center * lax.rsqrt(spread + 1e-5)
                gates = gb[h, at].astype(F32)
                silu = gates / (1.0 + jnp.exp(-gates))
                return (silu * normed).astype(BF16)

            def near_half():
                hid[tp, h] = hidden(mine)
                if h == 0:
                    for p in range(PIECES):
                        to_mate(h, p).start()

            def far_half():
                away[h] = hidden(1 - mine)
                for p in range(PIECES):
                    to_cross(h, p).start()

            for half in (near_half, far_half) if h == 0 else (far_half, near_half):
                half()

        def fold(source, h, at=slice(None), first=False):
            for slot in range(2):
                product = dot(hid[source, h, at], wov[slot, source, h * DH : (h + 1) * DH, :])
                oacc[slot, at] = product if first else oacc[slot, at] + product

        tok_copy(0).wait()
        own_product(KEY, 0)
        own_product(VALUE, 0)
        tok_copy(1).wait()
        key_value(0)
        states(0)
        key_value(1)
        states(1)
        query(0)
        wo_mate(0).wait_recv()
        wo_relay(0).start()
        many(arcv, asend, arecv).wait_recv()
        scan(0)
        gate(0)
        wo_mate(1).wait_recv()
        wo_relay(1).start()
        intra(0)
        scan(1)
        query(1)
        finish(0)

        wo_own().wait()
        wo_cross().wait_recv()
        for r in (tp, mate_tp, cross_tp):
            wo_hand(r).start()
        gate(1)
        intra(1)
        finish(1)
        for p in range(PIECES):
            to_cross(0, p).wait_recv()
            forward(0, p).start()
            to_mate(1, p).start()
            to_cross(1, p).wait_recv()
            forward(1, p).start()
            if p == 0:
                for part in range(2):
                    wo_relay(part).wait_recv()
                wo_hand(opposite_tp).start()
                wo_hand(tp).wait_recv()
                fold(tp, 0, first=True)
            if p == 1:
                fold(tp, 1)
            if p == 3:
                wo_hand(mate_tp).wait_recv()
                for q in range(PIECES):
                    to_mate(0, q).wait_recv()
                fold(mate_tp, 0)
        wo_hand(cross_tp).wait_recv()
        fold(cross_tp, 0)
        fold(cross_tp, 1)
        wo_hand(opposite_tp).wait_recv()

        def place(p):
            return pl.ds(pl.multiple_of(mine * BLOCK + p * PIECE, PIECE), PIECE)

        def give(p):
            return pltpu.make_async_remote_copy(
                src_ref=obuf.at[piece(p)], dst_ref=out.at[place(p)], send_sem=p2send.at[p],
                recv_sem=p2recv.at[p], device_id=cross,
            )

        for p in range(PIECES):
            forward(0, p).wait_recv()
            to_mate(1, p).wait_recv()
            forward(1, p).wait_recv()
            at = slice(p * PIECE, (p + 1) * PIECE)

            def total_of(slot):
                last = oacc[slot, at]
                for source, h in ((opposite_tp, 0), (mate_tp, 1), (opposite_tp, 1)):
                    rows_of = slice(h * DH, (h + 1) * DH)
                    last += dot(hid[source, h, at], wov[slot, source, rows_of, :])
                return last.astype(BF16)

            obuf[at] = total_of(1 - mine)
            give(p).start()
            out[place(p)] = total_of(mine)

        wo_cross().wait_send()
        for part in range(2):
            wo_mate(part).wait_send()
            wo_relay(part).wait_send()
        for r in range(n_tp):
            wo_hand(r).wait_send()
        for i, h in order:
            swap(i, h).wait_send()
        many(arcv, asend, arecv).wait_send()
        for h in range(2):
            many(rbuf.at[h], usend.at[h], urecv.at[h]).wait_send()
            many(sbuf.at[h], psend.at[h], precv.at[h]).wait_send()
            for p in range(PIECES):
                to_cross(h, p).wait_send()
                to_mate(h, p).wait_send()
                forward(h, p).wait_send()
        for p in range(PIECES):
            give(p).wait_send()
            give(p).wait_recv()

    return kernel


def solution(mesh):
    n_ctx, n_tp = mesh.shape["ctx"], mesh.shape["tp"]

    def on_device(tokens, query_weight, key_weight, value_weight, gate_weight, out_weight, log_decay):
        rows, depth = tokens.shape[1:]
        cols = query_weight.shape[1]
        out_rows = out_weight.shape[0]
        tables = rotation_rows(n_ctx, rows)
        vmem = lambda *shape, dtype=BF16: pltpu.VMEM(shape, dtype)
        dma = lambda *shape: pltpu.SemaphoreType.DMA(shape)
        anywhere = pl.BlockSpec(memory_space=pl.ANY)
        small = pl.BlockSpec(memory_space=pltpu.VMEM)
        result = pl.pallas_call(
            make_kernel(n_ctx, n_tp),
            out_shape=pltpu.VMEM((rows, cols), BF16),
            in_specs=[anywhere] * 8,
            out_specs=small,
            scratch_shapes=[
                vmem(cols // DH, rows, dtype=F32),
                vmem(*tables.shape, dtype=F32),
                vmem(rows, depth),
                vmem(4, 2, depth, DH),
                vmem(2, n_tp, out_rows, cols),
                vmem(2, rows, DH, dtype=F32),
                vmem(2, rows, DH),
                vmem(2, rows, DH),
                vmem(2, rows, DH),
                vmem(2, rows, DH),
                vmem(2, rows, DH, dtype=F32),
                vmem(2, 2, DH, DH, dtype=F32),
                vmem(2, n_ctx, 16, HALF),
                vmem(2, n_ctx, 16, HALF),
                vmem(2, n_ctx, 16, HALF),
                vmem(2, n_ctx, 16, HALF),
                vmem(8, HALF, dtype=F32),
                vmem(n_ctx, 8, HALF, dtype=F32),
                vmem(8, rows, dtype=F32),
                vmem(rows, 8, dtype=F32),
                vmem(rows, HALF, dtype=F32),
                vmem(rows, HALF, dtype=F32),
                vmem(2, DH, DH),
                vmem(n_tp, 2, BLOCK, DH),
                vmem(2, BLOCK, DH),
                vmem(2, BLOCK, cols, dtype=F32),
                vmem(BLOCK, cols),
                dma(2), dma(2), dma(4, 2), dma(4, 2), dma(4, 2), dma(), dma(),
                dma(2), dma(2), dma(2), dma(2),
                dma(), dma(5), dma(5), dma(n_tp), dma(n_tp),
                dma(2, PIECES), dma(2, PIECES), dma(2, PIECES), dma(2, PIECES),
                dma(2, PIECES), dma(2, PIECES), dma(PIECES), dma(PIECES),
            ],
            compiler_params=pltpu.CompilerParams(
                collective_id=0, has_side_effects=True, vmem_limit_bytes=60 << 20
            ),
            name="retention",
        )(
            tokens[0], key_weight, value_weight, query_weight, gate_weight, out_weight,
            jnp.transpose(log_decay[0]), tables,
        )
        return result[None]

    in_specs = (
        P("fsdp", "ctx", None),
        P("fsdp", "tp"),
        P("fsdp", "tp"),
        P("fsdp", "tp"),
        P("fsdp", "tp"),
        P("tp", "fsdp"),
        P("fsdp", "ctx", "tp"),
    )
    out_specs = P("fsdp", "ctx", "tp")
    return jax.shard_map(
        on_device, mesh=mesh, in_specs=in_specs, out_specs=out_specs, check_vma=False
    )
```

```python
import jax
import jax.numpy as jnp
import numpy as np
from jax import lax
from jax.experimental import pallas as pl
from jax.experimental.pallas import tpu as pltpu
from jax.sharding import PartitionSpec as P

DH = 256
HALF = DH // 2
BLOCK = 512
PIECES = 4
PIECE = BLOCK // PIECES
KEY, VALUE, QUERY, GATE = range(4)
F32, BF16 = jnp.float32, jnp.bfloat16


def dot(a, b):
    return jnp.dot(a, b, preferred_element_type=F32)


def rotation_rows(ctx_count, rows):
    frequency = 10000.0 ** (-np.arange(HALF) / HALF)
    tables = []
    for stride, count in ((32, rows // 32), (1, 32), (rows, ctx_count)):
        angles = (np.arange(count) * stride)[:, None] * frequency[None, :]
        tables += [np.cos(angles), np.sin(angles)]
    return np.concatenate(tables).astype(np.float32)


def make_kernel(n_ctx, n_tp):
    n_peers = n_ctx - 1

    def offset(i):
        return n_ctx // 2 + (i // 2 + lax.rem(i, 2)) * (1 - 2 * lax.rem(i, 2))

    def kernel(
        tok, wk, wv, wq, wg, wo, ld, turns, out,
        logs, table, tokv, wv_all, wov, acc, kb, vb, qb, gb, ret, ust, ubuf, rbuf, pbuf, sbuf,
        abuf, arcv, crow, ccol, cosv, sinv, stv, hid, away, oacc, obuf,
        isem, tsem, lsem, wsend, wrecv, asend, arecv, usend, urecv, psend, precv,
        wolocal, wosend, worecv, wofwd, wogot, crsend, crrecv, mtsend, mtrecv,
        fwsend, fwrecv, p2send, p2recv,
    ):
        ctx, tp, core = (lax.axis_index(n) for n in ("ctx", "tp", "fsdp"))
        rows = tok.shape[0]
        khalf = tok.shape[1] // 2
        partner = {"fsdp": 1 - core}
        mate_tp, cross_tp = tp + 1 - 2 * lax.rem(tp, 2), n_tp - 1 - tp
        opposite_tp = lax.rem(tp + 2, n_tp)
        mate, cross = {"tp": mate_tp}, {"tp": cross_tp}
        mine = tp // 2
        weights = (wk, wv, wq, wg)

        barrier = pltpu.get_barrier_semaphore()
        def greet(k, carry):
            pl.semaphore_signal(barrier, inc=1, device_id={"ctx": lax.rem(ctx + offset(k), n_ctx)})
            return carry

        lax.fori_loop(0, n_peers, greet, 0)
        pl.semaphore_signal(barrier, inc=1, device_id=partner)
        pl.semaphore_signal(barrier, inc=1, device_id=mate)
        pl.semaphore_signal(barrier, inc=1, device_id=cross)

        def log_copy():
            return pltpu.make_async_copy(ld, logs, isem.at[0])

        def table_copy():
            return pltpu.make_async_copy(turns, table, isem.at[1])

        log_copy().start()
        table_copy().start()

        own_rows = pl.ds(pl.multiple_of(core * khalf, khalf), khalf)
        other_rows = pl.ds(pl.multiple_of((1 - core) * khalf, khalf), khalf)

        def tok_copy(part):
            columns = own_rows if part == 0 else other_rows
            return pltpu.make_async_copy(tok.at[:, columns], tokv.at[:, columns], tsem.at[part])

        def own_copy(i, h):
            source = weights[i].at[:, h * DH : (h + 1) * DH]
            return pltpu.make_async_copy(source, wv_all.at[i, h, own_rows], lsem.at[i, h])

        order = [(KEY, 0), (VALUE, 0), (KEY, 1), (VALUE, 1), (QUERY, 0), (GATE, 0), (QUERY, 1), (GATE, 1)]
        tok_copy(0).start()
        for i, h in order[:2]:
            own_copy(i, h).start()
        tok_copy(1).start()
        for i, h in order[2:]:
            own_copy(i, h).start()

        crow[...] = jnp.zeros_like(crow)
        log_copy().wait()
        crow[0 : logs.shape[0], :] = logs[...]
        running = crow[...]
        lane = lax.rem(lax.broadcasted_iota(jnp.int32, running.shape, 1), BLOCK)
        step = 1
        while step < BLOCK:
            running = running + jnp.where(lane >= step, pltpu.roll(running, step, 1), 0.0)
            step *= 2
        crow[...] = running
        ccol[...] = running.T
        ends = [crow[:, (b + 1) * BLOCK - 1 : (b + 1) * BLOCK] for b in range(2)]
        total = ends[0] + ends[1]
        abuf[...] = jnp.broadcast_to(total, abuf.shape)
        arcv[ctx] = jnp.broadcast_to(total, abuf.shape)

        pl.semaphore_wait(barrier, 3 + n_peers)

        def swap(i, h):
            return pltpu.make_async_remote_copy(
                src_ref=weights[i].at[:, h * DH : (h + 1) * DH],
                dst_ref=wv_all.at[i, h, own_rows],
                send_sem=wsend.at[i, h],
                recv_sem=wrecv.at[i, h],
                device_id=partner,
            )

        for i, h in order:
            swap(i, h).start()

        def send_total(k, carry):
            pltpu.make_async_remote_copy(
                src_ref=abuf,
                dst_ref=arcv.at[ctx],
                send_sem=asend,
                recv_sem=arecv,
                device_id={"ctx": lax.rem(ctx + offset(k), n_ctx)},
            ).start()
            return carry

        lax.fori_loop(0, n_peers, send_total, 0)

        width = wo.shape[1] // 2
        group = lax.rem((tp + 1) // 2, 2)
        near = group + core * (1 - 2 * group)

        def wo_columns(index):
            return wo.at[:, pl.ds(pl.multiple_of(index * width, width), width)]

        def wo_own():
            return pltpu.make_async_copy(wo_columns(near), wov.at[core, tp], wolocal)

        def wo_copy(source, target, k, to):
            return pltpu.make_async_remote_copy(
                src_ref=source, dst_ref=target, send_sem=wosend.at[k],
                recv_sem=worecv.at[k], device_id=to,
            )

        def wo_cross():
            return wo_copy(wo_columns(near), wov.at[core, tp], 4, cross)

        part_rows = wo.shape[0] // 2

        def wo_mate(part):
            at = pl.ds(part * part_rows, part_rows)
            columns = pl.ds(pl.multiple_of((1 - near) * width, width), width)
            return wo_copy(wo.at[at, columns], wov.at[core, tp, at], part, mate)

        def wo_relay(part):
            block = wov.at[core, mate_tp, pl.ds(part * part_rows, part_rows)]
            return wo_copy(block, block, 2 + part, cross)

        def wo_hand(r):
            return pltpu.make_async_remote_copy(
                src_ref=wov.at[core, r], dst_ref=wov.at[core, r], send_sem=wofwd.at[r],
                recv_sem=wogot.at[r], device_id=partner,
            )

        wo_own().start()
        for part in range(2):
            wo_mate(part).start()
        wo_cross().start()

        table_copy().wait()
        fine = rows // 32
        cos_a, sin_a = table[0:fine, :], table[fine : 2 * fine, :]
        cos_b, sin_b = (table[2 * fine + k * 32 : 2 * fine + (k + 1) * 32, :] for k in range(2))
        base = 2 * fine + 64
        cc, sc = (table[pl.ds(base + k * n_ctx + ctx, 1), :] for k in range(2))
        base_cos, base_sin = cos_a * cc - sin_a * sc, sin_a * cc + cos_a * sc
        for a in range(rows // 32):
            ca, sa = base_cos[a : a + 1, :], base_sin[a : a + 1, :]
            cosv[a * 32 : (a + 1) * 32, :] = ca * cos_b - sa * sin_b
            sinv[a * 32 : (a + 1) * 32, :] = sa * cos_b + ca * sin_b

        def positions(b):
            return slice(b * BLOCK, (b + 1) * BLOCK)

        def own_product(i, h):
            own_copy(i, h).wait()
            acc[i] = dot(tokv[:, own_rows], wv_all[i, h, own_rows])

        def project(i, h, split=False):
            if split:
                swap(i, h).wait_recv()
                return acc[i] + dot(tokv[:, other_rows], wv_all[i, h, other_rows])
            own_copy(i, h).wait()
            swap(i, h).wait_recv()
            return dot(tokv[...], wv_all[i, h])

        def rotated(u):
            first, second = u[:, :HALF], u[:, HALF:]
            cosine, sine = cosv[...], sinv[...]
            return (first * cosine - second * sine).astype(BF16), (
                second * cosine + first * sine
            ).astype(BF16)

        def key_value(h):
            split = h == 0
            kb[h, :, :HALF], kb[h, :, HALF:] = rotated(project(KEY, h, split))
            vb[h] = project(VALUE, h, split).astype(BF16)

        def query(h):
            qb[h, :, :HALF], qb[h, :, HALF:] = rotated(project(QUERY, h))

        def gate(h):
            gb[h] = project(GATE, h).astype(BF16)

        def block_end(h, b):
            return crow[h : h + 1, (b + 1) * BLOCK - 1 : (b + 1) * BLOCK]

        def decay_column(h, b):
            return ccol[positions(b), h : h + 1]

        def states(h):
            for b in range(2):
                scale = jnp.exp(block_end(h, b) - decay_column(h, b))
                scaled = (kb[h, positions(b)].astype(F32) * scale).astype(BF16)
                ust[h, b] = lax.dot_general(
                    scaled, vb[h, positions(b)], (((0,), (0,)), ((), ())),
                    preferred_element_type=F32,
                )
            joined = (jnp.exp(block_end(h, 1)) * ust[h, 0] + ust[h, 1]).astype(BF16)
            for j in range(2):
                ubuf[h, j * 16 : (j + 1) * 16] = joined[:, j * HALF : (j + 1) * HALF].reshape(16, 16, HALF)
            rbuf[h, ctx] = ubuf[h, ctx]

            def send(k, carry):
                to = lax.rem(ctx + offset(k), n_ctx)
                pltpu.make_async_remote_copy(
                    src_ref=ubuf.at[h, to],
                    dst_ref=rbuf.at[h, ctx],
                    send_sem=usend.at[h],
                    recv_sem=urecv.at[h],
                    device_id={"ctx": to},
                ).start()
                return carry

            lax.fori_loop(0, n_peers, send, 0)

        def many(buffer, send_sem, recv_sem):
            part = buffer.at[pl.ds(0, n_peers)]
            return pltpu.make_async_remote_copy(
                src_ref=part, dst_ref=part, send_sem=send_sem, recv_sem=recv_sem,
                device_id={"ctx": lax.rem(ctx + 1, n_ctx)},
            )

        def scan(h):
            many(rbuf.at[h], usend.at[h], urecv.at[h]).wait_recv()

            before = jnp.zeros((16, HALF), F32)
            for d in range(n_ctx):
                pbuf[h, d] = before.astype(BF16)
                before = before * jnp.exp(arcv[d, h : h + 1, :]) + rbuf[h, d].astype(F32)
            sbuf[h, ctx] = pbuf[h, ctx]

            def send(k, carry):
                to = lax.rem(ctx + offset(k), n_ctx)
                pltpu.make_async_remote_copy(
                    src_ref=pbuf.at[h, to],
                    dst_ref=sbuf.at[h, ctx],
                    send_sem=psend.at[h],
                    recv_sem=precv.at[h],
                    device_id={"ctx": to},
                ).start()
                return carry

            lax.fori_loop(0, n_peers, send, 0)

        quarter = BLOCK // 2

        def intra(h):
            for b in range(2):
                for part in range(2):
                    start = b * BLOCK + part * quarter
                    extent = (part + 1) * quarter
                    mine = slice(start, start + quarter)
                    seen = slice(b * BLOCK, b * BLOCK + extent)
                    scores = lax.dot_general(
                        qb[h, mine], kb[h, seen], (((1,), (1,)), ((), ())),
                        preferred_element_type=F32,
                    )
                    t = lax.broadcasted_iota(jnp.int32, scores.shape, 0) + part * quarter
                    s = lax.broadcasted_iota(jnp.int32, scores.shape, 1)
                    differ = ccol[mine, h : h + 1] - crow[h : h + 1, seen]
                    decay = jnp.exp(jnp.where(t >= s, differ, 0.0))
                    mixed = jnp.where(t >= s, scores * decay, 0.0).astype(BF16)
                    ret[h, mine] = dot(mixed, vb[h, seen])

        def piece(p):
            return pl.ds(p * PIECE, PIECE)

        def hidden_copy(source, owner, h, p, sends, receives, to):
            return pltpu.make_async_remote_copy(
                src_ref=source, dst_ref=hid.at[owner, h, piece(p)], send_sem=sends.at[h, p],
                recv_sem=receives.at[h, p], device_id=to,
            )

        def to_cross(h, p):
            return hidden_copy(away.at[h, piece(p)], tp, h, p, crsend, crrecv, cross)

        def to_mate(h, p):
            return hidden_copy(hid.at[tp, h, piece(p)], tp, h, p, mtsend, mtrecv, mate)

        def forward(h, p):
            source = hid.at[cross_tp, h, piece(p)]
            return hidden_copy(source, cross_tp, h, p, fwsend, fwrecv, mate)

        def finish(h):
            many(sbuf.at[h], psend.at[h], precv.at[h]).wait_recv()
            state = jnp.concatenate(
                [sbuf[h, j * 16 : (j + 1) * 16].reshape(DH, HALF) for j in range(2)], axis=1
            )
            stv[0] = state
            stv[1] = (jnp.exp(block_end(h, 0)) * state.astype(F32) + ust[h, 0]).astype(BF16)

            def hidden(b):
                at = pl.ds(pl.multiple_of(b * BLOCK, BLOCK), BLOCK)
                inter = jnp.exp(ccol[at, h : h + 1]) * dot(qb[h, at], stv[b])
                retained = ret[h, at] + inter
                center = retained - jnp.mean(retained, axis=-1, keepdims=True)
                spread = jnp.mean(center * center, axis=-1, keepdims=True)
                normed = center * lax.rsqrt(spread + 1e-5)
                gates = gb[h, at].astype(F32)
                silu = gates / (1.0 + jnp.exp(-gates))
                return (silu * normed).astype(BF16)

            def near_half():
                hid[tp, h] = hidden(mine)
                if h == 0:
                    for p in range(PIECES):
                        to_mate(h, p).start()

            def far_half():
                away[h] = hidden(1 - mine)
                for p in range(PIECES):
                    to_cross(h, p).start()

            for half in (near_half, far_half) if h == 0 else (far_half, near_half):
                half()

        def fold(source, h, at=slice(None), first=False):
            for slot in range(2):
                product = dot(hid[source, h, at], wov[slot, source, h * DH : (h + 1) * DH, :])
                oacc[slot, at] = product if first else oacc[slot, at] + product

        tok_copy(0).wait()
        own_product(KEY, 0)
        own_product(VALUE, 0)
        tok_copy(1).wait()
        key_value(0)
        states(0)
        key_value(1)
        states(1)
        query(0)
        wo_mate(0).wait_recv()
        wo_relay(0).start()
        many(arcv, asend, arecv).wait_recv()
        scan(0)
        gate(0)
        wo_mate(1).wait_recv()
        wo_relay(1).start()
        intra(0)
        scan(1)
        query(1)
        finish(0)

        wo_own().wait()
        wo_cross().wait_recv()
        for r in (tp, mate_tp, cross_tp):
            wo_hand(r).start()
        gate(1)
        intra(1)
        finish(1)
        ahead = PIECES // 2
        for p in range(ahead):
            to_cross(0, p).wait_recv()
            forward(0, p).start()
        wo_hand(tp).wait_recv()
        fold(tp, 0, first=True)
        for p in range(PIECES):
            if p + ahead < PIECES:
                to_cross(0, p + ahead).wait_recv()
                forward(0, p + ahead).start()
            to_mate(1, p).start()
            to_cross(1, p).wait_recv()
            forward(1, p).start()
            if p == 0:
                for part in range(2):
                    wo_relay(part).wait_recv()
                wo_hand(opposite_tp).start()
            if p == 1:
                fold(tp, 1)
            if p == 3:
                wo_hand(mate_tp).wait_recv()
                for q in range(PIECES):
                    to_mate(0, q).wait_recv()
                fold(mate_tp, 0)
        wo_hand(cross_tp).wait_recv()
        fold(cross_tp, 0)
        fold(cross_tp, 1)
        wo_hand(opposite_tp).wait_recv()

        def place(p):
            return pl.ds(pl.multiple_of(mine * BLOCK + p * PIECE, PIECE), PIECE)

        def give(p):
            return pltpu.make_async_remote_copy(
                src_ref=obuf.at[piece(p)], dst_ref=out.at[place(p)], send_sem=p2send.at[p],
                recv_sem=p2recv.at[p], device_id=cross,
            )

        for p in range(PIECES):
            forward(0, p).wait_recv()
            to_mate(1, p).wait_recv()
            forward(1, p).wait_recv()
            at = slice(p * PIECE, (p + 1) * PIECE)

            def total_of(slot):
                last = oacc[slot, at]
                for source, h in ((opposite_tp, 0), (mate_tp, 1), (opposite_tp, 1)):
                    rows_of = slice(h * DH, (h + 1) * DH)
                    last += dot(hid[source, h, at], wov[slot, source, rows_of, :])
                return last.astype(BF16)

            obuf[at] = total_of(1 - mine)
            give(p).start()
            out[place(p)] = total_of(mine)

        wo_cross().wait_send()
        for part in range(2):
            wo_mate(part).wait_send()
            wo_relay(part).wait_send()
        for r in range(n_tp):
            wo_hand(r).wait_send()
        for i, h in order:
            swap(i, h).wait_send()
        many(arcv, asend, arecv).wait_send()
        for h in range(2):
            many(rbuf.at[h], usend.at[h], urecv.at[h]).wait_send()
            many(sbuf.at[h], psend.at[h], precv.at[h]).wait_send()
            for p in range(PIECES):
                to_cross(h, p).wait_send()
                to_mate(h, p).wait_send()
                forward(h, p).wait_send()
        for p in range(PIECES):
            give(p).wait_send()
            give(p).wait_recv()

    return kernel


def solution(mesh):
    n_ctx, n_tp = mesh.shape["ctx"], mesh.shape["tp"]

    def on_device(tokens, query_weight, key_weight, value_weight, gate_weight, out_weight, log_decay):
        rows, depth = tokens.shape[1:]
        cols = query_weight.shape[1]
        out_rows = out_weight.shape[0]
        tables = rotation_rows(n_ctx, rows)
        vmem = lambda *shape, dtype=BF16: pltpu.VMEM(shape, dtype)
        dma = lambda *shape: pltpu.SemaphoreType.DMA(shape)
        anywhere = pl.BlockSpec(memory_space=pl.ANY)
        small = pl.BlockSpec(memory_space=pltpu.VMEM)
        result = pl.pallas_call(
            make_kernel(n_ctx, n_tp),
            out_shape=pltpu.VMEM((rows, cols), BF16),
            in_specs=[anywhere] * 8,
            out_specs=small,
            scratch_shapes=[
                vmem(cols // DH, rows, dtype=F32),
                vmem(*tables.shape, dtype=F32),
                vmem(rows, depth),
                vmem(4, 2, depth, DH),
                vmem(2, n_tp, out_rows, cols),
                vmem(2, rows, DH, dtype=F32),
                vmem(2, rows, DH),
                vmem(2, rows, DH),
                vmem(2, rows, DH),
                vmem(2, rows, DH),
                vmem(2, rows, DH, dtype=F32),
                vmem(2, 2, DH, DH, dtype=F32),
                vmem(2, n_ctx, 16, HALF),
                vmem(2, n_ctx, 16, HALF),
                vmem(2, n_ctx, 16, HALF),
                vmem(2, n_ctx, 16, HALF),
                vmem(8, HALF, dtype=F32),
                vmem(n_ctx, 8, HALF, dtype=F32),
                vmem(8, rows, dtype=F32),
                vmem(rows, 8, dtype=F32),
                vmem(rows, HALF, dtype=F32),
                vmem(rows, HALF, dtype=F32),
                vmem(2, DH, DH),
                vmem(n_tp, 2, BLOCK, DH),
                vmem(2, BLOCK, DH),
                vmem(2, BLOCK, cols, dtype=F32),
                vmem(BLOCK, cols),
                dma(2), dma(2), dma(4, 2), dma(4, 2), dma(4, 2), dma(), dma(),
                dma(2), dma(2), dma(2), dma(2),
                dma(), dma(5), dma(5), dma(n_tp), dma(n_tp),
                dma(2, PIECES), dma(2, PIECES), dma(2, PIECES), dma(2, PIECES),
                dma(2, PIECES), dma(2, PIECES), dma(PIECES), dma(PIECES),
            ],
            compiler_params=pltpu.CompilerParams(
                collective_id=0, has_side_effects=True, vmem_limit_bytes=60 << 20
            ),
            name="retention",
        )(
            tokens[0], key_weight, value_weight, query_weight, gate_weight, out_weight,
            jnp.transpose(log_decay[0]), tables,
        )
        return result[None]

    in_specs = (
        P("fsdp", "ctx", None),
        P("fsdp", "tp"),
        P("fsdp", "tp"),
        P("fsdp", "tp"),
        P("fsdp", "tp"),
        P("tp", "fsdp"),
        P("fsdp", "ctx", "tp"),
    )
    out_specs = P("fsdp", "ctx", "tp")
    return jax.shard_map(
        on_device, mesh=mesh, in_specs=in_specs, out_specs=out_specs, check_vma=False
    )
```
